32 devices in a mesh: head: 2 (over x), seq: 16 (over z, y, core).
Axes of the slice: x: 2, y: 2, z: 4, core: 2. Of those that a mesh axis runs over, the one named last changes fastest.
Arguments:
- query_rows: bfloat16 [16, 2, 256, 256], P('seq', 'head'), may hold values from -6 to 6
- key_rows: bfloat16 [16, 2, 256, 256], P('seq', 'head'), may hold values from -6 to 6
- value_rows: bfloat16 [16, 2, 256, 256], P('seq', 'head'), may hold values from -6 to 6
- output_grad: bfloat16 [16, 2, 256, 256], P('seq', 'head'), may hold values from -384 to 384
- output_rows: bfloat16 [16, 2, 256, 256], P('seq', 'head'), may hold values from -1.5 to 1.5
- row_logsumexp: float32 [8192, 2], P('seq', 'head')
- chosen_owner: int32 [128, 2], P('seq'), may hold values from 0 to 15, all different within a row; in each aligned block of 8 rows (0 to 7, 8 to 15, ...) at most 2 rows name the same one
- chosen_cubes: int32 [128, 2, 8], P('seq'), may hold values 0 or 1
Outputs:
- query_grad: bfloat16 [16, 2, 256, 256], P('seq', 'head')
- key_grad: bfloat16 [16, 2, 256, 256], P('seq', 'head')
- value_grad: bfloat16 [16, 2, 256, 256], P('seq', 'head')
The draws below stay inside these ranges and needn't reach their ends.
Inputs may be any that keep to these rules, and one draw needn't show every extreme that they name: `chosen_owner`: each query cube names 2 different indices; the 8 query cubes held by one index of seq name any one index at most 2 times, and exactly 2 times for some index in every draw. `chosen_cubes`: 1 marks a selected key cube.
All inputs are finite; a program needn't handle non-finite values. No bound on the sum of `chosen_cubes` on one device may be relied on, other than what follows from the above.
Results may differ from the reference program's by a relative error of at most 0.0053.
Values may be sent and summed in bfloat16 or wider, within the bound.
A program may use at most 64 MiB of HBM per device.

```python
import math
import jax
import jax.numpy as jnp
import numpy as np
from jax import lax

HD = 128
CUBE = 64
CUBE_DEV = 8
CAP = 2
SEL = 2
HEADS = 2
TOK_DEV = 512
TOKENS = 8192
NQC = 128
PIECE = 256
N_HEAD = 2
N_SEQ = 16


def draw_row_logsumexp(key, part):
    centre = jnp.log(jnp.float32(SEL * CUBE_DEV * CUBE) * 0.5) + 0.5
    spread = 0.3 * jnp.clip(jax.random.normal(key, (TOKENS, HEADS), jnp.float32), -6.0, 6.0)
    return centre + spread


def touch_ends(values, rng, low, largest):
    extent = values.shape
    index_at = [jax.random.randint(jax.random.fold_in(rng, axis), (), 0, extent[axis]) for axis in range(len(extent))]
    values = values.at[tuple(index_at)].set(low)
    longest = extent.index(max(extent))
    index_at[longest] = (index_at[longest] + 1) % extent[longest]
    return values.at[tuple(index_at)].set(largest)


def steps_of(stream_key, dims, shards, least, high):
    gain = 1.0
    for position, shards_of in shards:
        steps = jax.random.uniform(jax.random.fold_in(jax.random.fold_in(stream_key, 6), position), (shards_of,), jnp.float32, least / len(shards), high / len(shards))
        gain = gain * jnp.repeat(jnp.exp(steps), dims[position] // shards_of).reshape((-1,) + (1,) * (len(dims) - 1 - position))
    return gain


def routed_block(rng, own, number, rows, amount, top, most, lean):
    sequence = jax.random.permutation(rng, amount)
    heavy_load, usual = shares(amount, rows * top, most, lean, True), shares(amount, rows * top, most, lean, False)
    places = jnp.arange(amount)

    def named(tallies, turn):
        used = int((tallies > 0).sum())
        fixed = max(1, used // 4)
        shifted = fixed + (places - fixed + turn * (used - fixed)) % max(1, amount - fixed)
        return jnp.zeros((amount,), jnp.int32).at[sequence[jnp.where(places < fixed, places, shifted)]].set(jnp.asarray(tallies, jnp.int32))

    tallies = jnp.where(number % 4 == 0, named(heavy_load, number // 4), named(usual, number - number // 4 - 1))
    mixed = jax.random.permutation(jax.random.fold_in(own, 3), amount)
    donor, sink = mixed[0:amount // 2 * 2:2], mixed[1:amount // 2 * 2:2]
    margin = jnp.minimum(tallies[donor] - 1, most - tallies[sink]) // 2
    margin = jnp.where((donor == sequence[0]) | (sink == sequence[0]) | (tallies[sink] == 0), 0, jnp.maximum(margin, 0))
    shifted = jax.random.randint(jax.random.fold_in(own, 4), (amount // 2,), 0, 1 << 20) % (margin + 1)
    tallies = tallies.at[donor].add(-shifted).at[sink].add(shifted)
    labels = jnp.searchsorted(jnp.cumsum(tallies), jnp.arange(rows * top), side="right").astype(jnp.int32)
    table = labels.reshape(top, rows).T
    table = table[jax.random.permutation(jax.random.fold_in(own, 1), rows)]
    turn = jax.random.randint(jax.random.fold_in(own, 2), (rows, 1), 0, top)
    return jnp.take_along_axis(table, (jnp.arange(top)[None, :] + turn) % top, axis=1)


def shares(count, total, limit, lean, full):
    loads = [(1 << 20) // math.isqrt(grade ** lean) + 1 for grade in range(1, count + 1)]
    largest = limit if full else min(limit, max(-(-total // count), total * loads[0] // sum(loads)))
    least = 1 if total - largest >= count - 1 else 0
    holding, spare = [largest] + [least] * (count - 1), total - largest - least * (count - 1)
    while spare > 0:
        free = [i for i in range(1, count) if holding[i] < largest] or [i for i in range(1, count) if holding[i] < limit]
        pool, left = sum([loads[i] for i in free]), spare
        for i in free:
            more = min(limit - holding[i], max(1, left * loads[i] // pool), spare)
            holding[i] = holding[i] + more
            spare = spare - more
    return np.array(holding)


def centred(own_key, extent, scale, bound, split=(), kind=jnp.bfloat16):
    entries = scale * jax.random.normal(own_key, extent, jnp.float32)
    if split:
        entries = entries * steps_of(own_key, extent, split, -0.22, 0.18)
    return jnp.clip(entries, -bound, bound).astype(kind)


def setup_inputs(seed: int = 0) -> dict:
    seeds = jax.random.split(jax.random.key(seed), 9)
    query_rows = centred(seeds[0], (N_SEQ, N_HEAD, PIECE, HEADS * HD), 1.0, 6.0, ((0, 16), (1, 2)))
    key_rows = centred(seeds[1], (N_SEQ, N_HEAD, PIECE, HEADS * HD), 1.0, 6.0, ((0, 16), (1, 2)))
    value_rows = centred(seeds[2], (N_SEQ, N_HEAD, PIECE, HEADS * HD), 1.0, 6.0, ((0, 16), (1, 2)))
    output_grad = centred(seeds[3], (N_SEQ, N_HEAD, PIECE, HEADS * HD), 64.0, 384.0, ((0, 16), (1, 2)))
    output_rows = centred(seeds[4], (N_SEQ, N_HEAD, PIECE, HEADS * HD), 0.25, 1.5, ((0, 16), (1, 2)))
    row_logsumexp = draw_row_logsumexp(jax.random.fold_in(seeds[8], 71), 0)
    chosen_owner_keys = jax.random.split(jax.random.fold_in(seeds[6], 1), NQC // CUBE_DEV)
    chosen_owner_turns = jax.random.permutation(jax.random.fold_in(seeds[6], 3), NQC // CUBE_DEV)
    chosen_owner = jax.vmap(lambda own, number: routed_block(jax.random.fold_in(seeds[6], 2), own, number, CUBE_DEV, N_SEQ, SEL, CAP, 2))(chosen_owner_keys, chosen_owner_turns).reshape((NQC, SEL))
    chosen_cubes = touch_ends((jax.random.randint(seeds[7], (NQC, SEL, CUBE_DEV), 0, 2) < 1).astype(jnp.int32), jax.random.fold_in(seeds[7], 1), 0, 1)
    return dict(query_rows=query_rows, key_rows=key_rows, value_rows=value_rows, output_grad=output_grad, output_rows=output_rows, row_logsumexp=row_logsumexp, chosen_owner=chosen_owner, chosen_cubes=chosen_cubes)


def reference(query_rows, key_rows, value_rows, output_grad, output_rows, row_logsumexp, chosen_owner, chosen_cubes):

    def to_heads(array):
        return array.reshape(TOKENS, HEADS, HD).transpose(1, 0, 2)
    softmax_scale = 1.0 / math.sqrt(HD)
    cube_group = 8
    block_count = NQC // cube_group
    owners = chosen_owner.astype(jnp.int32).reshape(block_count, cube_group, SEL)
    masks = chosen_cubes.astype(jnp.float32).reshape(block_count, cube_group, SEL, CUBE_DEV)

    def one_head(head_arrays):
        query_head, key_head, value_head, grad_head, output_head, log_head = head_arrays
        row_delta = lax.optimization_barrier(jnp.sum(grad_head.astype(jnp.float32) * output_head.astype(jnp.float32), axis=-1))
        key_blocks = key_head.reshape(N_SEQ, TOK_DEV, HD)
        value_blocks = value_head.reshape(N_SEQ, TOK_DEV, HD)

        def cube_step(totals, cube_block):
            grad_k, grad_v = totals
            owner_part, mask_part, query_part, grad_part, log_part, delta_part = cube_block
            key_sel = jnp.take(key_blocks, owner_part, axis=0).astype(jnp.float32)
            value_sel = jnp.take(value_blocks, owner_part, axis=0).astype(jnp.float32)
            query_wide = query_part.astype(jnp.float32)
            grad_wide = grad_part.astype(jnp.float32)
            scores = jnp.einsum('crd,cjkd->cjrk', query_wide, key_sel) * softmax_scale
            key_keep = jnp.repeat(mask_part, CUBE, axis=-1)
            weights = jnp.exp(scores - log_part[:, None, :, None]) * key_keep[:, :, None, :]
            dweights = jnp.einsum('crd,cjkd->cjrk', grad_wide, value_sel)
            dscores = weights * (dweights - delta_part[:, None, :, None])
            weights_low = lax.optimization_barrier(weights.astype(jnp.bfloat16)).astype(jnp.float32)
            dscores_low = lax.optimization_barrier(dscores.astype(jnp.bfloat16)).astype(jnp.float32)
            value_terms = jnp.einsum('cjrk,crd->cjkd', weights_low, grad_wide)
            key_terms = softmax_scale * jnp.einsum('cjrk,crd->cjkd', dscores_low, query_wide)
            query_terms = softmax_scale * jnp.einsum('cjrk,cjkd->crd', dscores_low, key_sel)
            flat_owner = owner_part.reshape(-1)
            grad_k = grad_k.at[flat_owner].add(key_terms.reshape(-1, TOK_DEV, HD))
            grad_v = grad_v.at[flat_owner].add(value_terms.reshape(-1, TOK_DEV, HD))
            return ((grad_k, grad_v), query_terms)
        zero_init = jnp.zeros((N_SEQ, TOK_DEV, HD), jnp.float32)
        inputs = (owners, masks, query_head.reshape(block_count, cube_group, CUBE, HD), grad_head.reshape(block_count, cube_group, CUBE, HD), log_head.reshape(block_count, cube_group, CUBE), row_delta.reshape(block_count, cube_group, CUBE))
        (grad_k, grad_v), query_terms = lax.scan(cube_step, (zero_init, zero_init), inputs)
        return (query_terms.reshape(TOKENS, HD), grad_k.reshape(TOKENS, HD), grad_v.reshape(TOKENS, HD))
    head_inputs = (to_heads(query_rows), to_heads(key_rows), to_heads(value_rows), to_heads(output_grad), to_heads(output_rows), row_logsumexp.transpose(1, 0))
    grad_q, grad_k, grad_v = lax.map(one_head, head_inputs)

    def to_rows(array):
        return array.transpose(1, 0, 2).reshape(N_SEQ, N_HEAD, PIECE, HEADS * HD).astype(jnp.bfloat16)
    return (to_rows(grad_q), to_rows(grad_k), to_rows(grad_v))
```

```python
import functools
import math

import jax
import jax.numpy as jnp
from jax import lax
from jax.experimental import pallas as pl
from jax.experimental.pallas import tpu as pltpu
from jax.sharding import PartitionSpec as P

CAP = 2
PAIR = 2
SHARE = 2
LOG2E = math.log2(math.e)
NT = (((1,), (1,)), ((), ()))
NN = (((1,), (0,)), ((), ()))


def kernel(
    heads, seqs, sel,
    pick_ref, table_ref, q_ref, k_ref, v_ref, g_ref, o_ref, lse_ref,
    retq_ref, retkv_ref,
    qb, kv, kt, g_all, o_all, dsend, dlt, base, meta, tab, tab_s,
    slot, ret_ix, wq, wm, wy, wym, dk, dv, own_dq, give, got, wr, fin, skv,
    ys, ym, yr, yrm, yd, yq,
    loc_sem, qx_s, qn_s, qg_s, q_r, qc_s, qc_r, mn_s, mg_s, m_r, mc_s, mc_r,
    t_s, t_r, tc_s, tc_r, dl_s, dl_r, kv_s, kv_r, gv_s, gv_r, fq_s, fq_r, fk_s, fk_r,
    ys_s, ys_r, ym_s, ym_r, yd_s, yd_r,
):
    h = lax.axis_index("head")
    s = lax.axis_index("seq")
    group = PAIR * SHARE
    line = seqs // group
    z = s // group
    y = (s // PAIR) % SHARE
    c = s % PAIR
    side_len = line // 2
    ends = side_len - 1
    side = z // side_len
    first = side * side_len
    _, _, _, _, piece, rows, width = qb.shape
    cubes = heads * piece
    keys = cubes * rows
    wide = CAP * rows
    metas = meta.shape[3]
    scale = 1.0 / math.sqrt(width)
    gate_here = (1 - side) * (side_len - 1) + side * side_len
    gate_far = (1 - side) * side_len + side * (side_len - 1)
    is_gate = z == gate_here
    is_end = z != gate_here
    owners = 2 + ends
    finds = owners + 2 * ends
    own_slots = owners * CAP
    zero_slot = 2 * own_slots + 2 * ends * CAP

    def dev(hh, zz, yy, cc):
        return {"head": hh, "seq": zz * group + yy * PAIR + cc}

    def near(t):
        return first + (z - first + t) % side_len

    def source(t):
        is_far = t // side_len
        k = t - side_len
        far = (1 - side) * (side_len + k) + side * (side_len - 1 - k)
        return (1 - is_far) * near(t) + is_far * far

    def other(t):
        return (h + t) % heads

    barrier = pltpu.get_barrier_semaphore()
    for t in range(heads):
        pl.semaphore_signal(barrier, inc=1, device_id=dev(other(t), z, 1 - y, c))
        for m in range(line):
            if t or m:
                pl.semaphore_signal(barrier, inc=1, device_id=dev(other(t), (z + m) % line, y, c))
    pl.semaphore_signal(barrier, inc=1, device_id=dev(h, z, y, 1 - c))
    pl.semaphore_signal(barrier, inc=1, device_id=dev(h, z, 1 - y, 1 - c))
    partners = heads + heads * line + 1

    def cols(a):
        return pl.ds(pl.multiple_of(a * width, width), width)

    def rows_of(a):
        return pl.ds(a * piece, piece)

    loads = [pltpu.make_async_copy(g_ref, g_all, loc_sem.at[0]),
             pltpu.make_async_copy(o_ref, o_all, loc_sem.at[1])]
    stage = []
    for n, (a, b) in enumerate(((q_ref, k_ref), (g_ref, v_ref))):
        stage.append(pltpu.make_async_copy(a.at[:, :, cols(h)], qb.at[0, z, h, n], loc_sem.at[2 + n]))
        stage.append(pltpu.make_async_copy(b.at[:, :, cols(h)], kv.at[0, h, n], loc_sem.at[4 + n]))
    for d in loads + stage:
        d.start()

    pl.semaphore_wait(barrier, partners)

    def remote(src, dst, send, recv, to):
        return pltpu.make_async_remote_copy(
            src_ref=src, dst_ref=dst, send_sem=send, recv_sem=recv, device_id=to)

    def hop(m):
        return gate_far if m == 0 else near(m)

    def q_own(p, m):
        return remote(qb.at[0, z, p], qb.at[0, z, p], qn_s.at[p, m], q_r.at[z, p], dev(h, hop(m), y, c))

    def q_relay(zz, p):
        return remote(qb.at[0, zz, p], qb.at[0, zz, p], qg_s.at[zz, p], q_r.at[zz, p], dev(h, gate_far, y, c))

    def q_cross(t):
        a = other(t)
        return remote(qb.at[0, z, a], qb.at[0, z, h], qx_s.at[t], q_r.at[z, h], dev(a, z, y, c))

    def q_core(zz, p):
        return remote(qb.at[0, zz, p], qb.at[1, zz, p], qc_s.at[zz, p], qc_r.at[zz, p], dev(h, z, y, 1 - c))

    def m_own(m):
        return remote(meta.at[0, z], meta.at[0, z], mn_s.at[m], m_r.at[z], dev(h, hop(m), y, c))

    def m_relay(zz):
        return remote(meta.at[0, zz], meta.at[0, zz], mg_s.at[zz], m_r.at[zz], dev(h, gate_far, y, c))

    def m_core(zz):
        return remote(meta.at[0, zz], meta.at[1, zz], mc_s.at[zz], mc_r.at[zz], dev(h, z, y, 1 - c))

    def t_line(m):
        return remote(table_ref, tab.at[0, z], t_s.at[m], t_r.at[z], dev(h, (z + m) % line, y, c))

    def t_from(zz):
        return remote(table_ref, tab.at[0, zz], t_s.at[0], t_r.at[zz], dev(h, zz, y, c))

    t_core = remote(tab.at[0], tab.at[1], tc_s.at[0], tc_r.at[0], dev(h, z, y, 1 - c))

    def d_cross(t):
        a = other(t)
        return remote(dsend.at[a], dlt.at[rows_of(h)], dl_s.at[t], dl_r.at[h], dev(a, z, y, c))

    def d_from(a):
        return remote(dsend.at[a], dlt.at[rows_of(a)], dl_s.at[0], dl_r.at[a], dev(a, z, y, c))

    def kv_done(t, o):
        return remote(kv.at[0, h], kv.at[o, h], kv_s.at[t, o], kv_r.at[o, h], dev(other(t), z, 1 - y, c))

    def kv_from(a, o):
        return remote(kv.at[0, h], kv.at[o, a], kv_s.at[0, 0], kv_r.at[o, a], dev(h, z, 1 - y, c))

    def give_copy(zz, count):
        part = pl.ds(0, count)
        return remote(give.at[zz, part], got.at[zz, part], gv_s.at[zz], gv_r.at[zz], dev(h, z, y, 1 - c))

    def fq_copy(t, zz, at):
        a = other(t)
        return remote(fin.at[zz, a], retq_ref.at[at, h], fq_s.at[zz, t], fq_r.at[at, h], dev(a, zz, y, c))

    def fq_from(at, a):
        return remote(fin.at[z, a], retq_ref.at[at, a], fq_s.at[0, 0], fq_r.at[at, a], dev(a, gate_far, y, c))

    def fk_copy(t, o):
        a = other(t)
        if o < 2:
            return remote(skv.at[o, a], retkv_ref.at[o, h], fk_s.at[o, t], fk_r.at[o, h], dev(a, z, (y + o) % SHARE, c))
        return remote(skv.at[o, a], retkv_ref.at[2, h], fk_s.at[o, t], fk_r.at[2, h], dev(a, near(o - 1), y, c))

    def fk_from(a, o):
        return remote(skv.at[o, a], retkv_ref.at[o, a], fk_s.at[0, 0], fk_r.at[o, a], dev(a, gate_far, y, c))

    def y_copy(k, m, cc):
        return (
            remote(ys.at[k, m, cc], yr.at[k, m, c], ys_s.at[k, m, cc], ys_r.at[k, m, c], dev(h, z, 1 - y, cc)),
            remote(ym.at[k, m, cc], yrm.at[k, m, c], ym_s.at[k, m, cc], ym_r.at[k, m, c], dev(h, z, 1 - y, cc)),
        )

    def y_from(k, m, cc):
        return (
            remote(ys.at[k, m, cc], yr.at[k, m, cc], ys_s.at[k, m, cc], ys_r.at[k, m, cc], dev(h, z, 1 - y, cc)),
            remote(ym.at[k, m, cc], yrm.at[k, m, cc], ym_s.at[k, m, cc], ym_r.at[k, m, cc], dev(h, z, 1 - y, cc)),
        )

    def y_back(k, m, cc):
        return remote(yd.at[k, m, cc], yq.at[k, m, c], yd_s.at[k, m, cc], yd_r.at[k, m, c], dev(h, z, 1 - y, cc))

    def y_done(k, m, cc):
        return remote(yd.at[k, m, cc], yq.at[k, m, cc], yd_s.at[k, m, cc], yd_r.at[k, m, cc], dev(h, z, 1 - y, cc))

    def send_parts(srcs, dst, send, recv, a, to):
        for n, src in enumerate(srcs):
            remote(src.at[:, :, cols(a)], dst.at[n], send, recv, to).start()

    def first_part(m):
        send_parts((q_ref, g_ref), qb.at[0, z, h], qn_s.at[h, m], q_r.at[z, h], h, dev(h, hop(m), y, c))

    for m in range(1, line):
        t_line(m).start()

    @pl.when(is_gate)
    def _():
        first_part(0)

    for m in range(1, side_len):
        first_part(m)
    for t in range(1, heads):
        send_parts((q_ref, g_ref), qb.at[0, z, h], qx_s.at[t], q_r.at[z, h], other(t), dev(other(t), z, y, c))
    send_parts((q_ref, g_ref), qb.at[1, z, h], qc_s.at[z, h], qc_r.at[z, h], h, dev(h, z, y, 1 - c))

    row = lax.broadcasted_iota(jnp.int32, (metas, wide), 0)
    lane = lax.broadcasted_iota(jnp.int32, (3, wide), 1)
    for d in loads:
        d.wait()
    for a in range(heads):
        for x in range(piece):
            prod = g_all[x, :, a * width:(a + 1) * width].astype(jnp.float32) * o_all[
                x, :, a * width:(a + 1) * width
            ].astype(jnp.float32)
            both = jnp.concatenate([prod] * CAP, axis=0)
            total = jnp.sum(both.T, axis=0, keepdims=True)
            dsend[a, x] = jnp.where(row == 1, jnp.broadcast_to(total, (metas, wide)), 0.0)
    for t in range(1, heads):
        d_cross(t).start()
    for t in range(heads):
        for o in (1, 0):
            if t or o:
                send_parts((k_ref, v_ref), kv.at[o, h], kv_s.at[t, o], kv_r.at[o, h], other(t),
                           dev(other(t), z, (y + o) % SHARE, c))

    for x in range(cubes):
        line_x = jnp.concatenate([lse_ref[:, x * rows:(x + 1) * rows] * LOG2E] * CAP, axis=1)
        both = jnp.where(row == 0, jnp.broadcast_to(line_x, (metas, wide)), 0.0)
        for j in range(sel):
            bits = jnp.int32(0)
            for k in range(cubes):
                bits = bits + jnp.where(pick_ref[x, j, k] != 0, 1 << k, 0)
            both = jnp.where(row == 2 + j, bits.astype(jnp.float32), both)
        base[x] = both
    tab[0, z] = table_ref[...]
    dlt[rows_of(h)] = dsend[h]
    for d in stage:
        d.wait()

    def recv_part(t, i, relays):
        zz = source(t)
        p = other(i)
        q_relay(zz, p).wait_recv()
        if relays:
            q_relay(zz, p).start()
        q_core(zz, p).start()

    def recv_meta(t, relays):
        zz = source(t)
        m_relay(zz).wait_recv()
        if relays:
            m_relay(zz).start()
        m_core(zz).start()

    @pl.when(is_gate)
    def _():
        for t in range(1, side_len):
            recv_part(t, 0, True)

    for t in range(1, heads):
        q_relay(z, other(t)).wait_recv()

        @pl.when(is_gate)
        def _():
            q_own(other(t), 0).start()

        for m in range(1, side_len):
            q_own(other(t), m).start()
        q_core(z, other(t)).start()

    for t in range(1, heads):
        d_from(other(t)).wait_recv()
    for x in range(cubes):
        meta[0, z, x] = base[x] + dlt[x]

    @pl.when(is_gate)
    def _():
        m_own(0).start()

    for m in range(1, side_len):
        m_own(m).start()
    m_core(z).start()

    @pl.when(is_end)
    def _():
        at = 1 + (z - gate_here + side_len) % side_len
        for t in range(heads):
            send_parts((k_ref, v_ref), kv.at[at, h], kv_s.at[t, 2], kv_r.at[at, h], other(t),
                       dev(other(t), gate_here, y, c))

    @pl.when(is_gate)
    def _():
        for t in range(1, side_len):
            for i in range(1, heads):
                recv_part(t, i, True)
            recv_meta(t, True)

    dk[...] = jnp.zeros_like(dk)
    dv[...] = jnp.zeros_like(dv)
    wr[zero_slot] = jnp.zeros_like(wr[zero_slot])

    for m in range(1, line):
        t_from((z + m) % line).wait_recv()
    t_core.start()

    @pl.when(is_end)
    def _():
        for t in range(1, side_len):
            for i in range(heads):
                recv_part(t, i, False)
            recv_meta(t, False)

    t_core.wait_recv()
    to_smem = pltpu.make_async_copy(tab, tab_s, loc_sem.at[0])
    to_smem.start()
    to_smem.wait()

    def number(zz, yy, cc):
        return zz * group + yy * PAIR + cc

    mine = [number(z, y, c), number(z, 1 - y, c)]
    mine = mine + [number(near(m), y, c) for m in range(1, side_len)]
    across = [number(near(m), 1 - y, cc) for m in range(1, side_len) for cc in range(PAIR)]
    theirs = [number(z, y, 1 - c), number(z, 1 - y, 1 - c)]
    theirs = theirs + [number(near(m), y, 1 - c) for m in range(1, side_len)]

    def find(zz, l, who):
        for o, d in who:
            found = [jnp.int32(-1)] * CAP
            for e in range(cubes * sel - 1, -1, -1):
                hit = tab_s[l, zz, e % sel, e // sel] == d
                for k in range(CAP - 1, 0, -1):
                    found[k] = jnp.where(hit, found[k - 1], found[k])
                found[0] = jnp.where(hit, e, found[0])
            for k in range(CAP):
                slot[((zz * 2 + l) * finds + o) * CAP + k] = found[k]

    def rank(zz, who):
        count = [jnp.int32(0)] * len(who)
        for e in range(cubes * sel):
            d = tab_s[0, zz, e % sel, e // sel]
            ix = jnp.int32(zero_slot)
            for n, (at, d_n) in enumerate(who):
                hit = d == d_n
                ix = jnp.where(hit, at + jnp.minimum(count[n], CAP - 1), ix)
                count[n] = count[n] + hit.astype(jnp.int32)
            ret_ix[zz * cubes * sel + e] = ix

    @pl.loop(0, side_len)
    def _(t):
        zz = source(t)
        for l in range(2):
            find(zz, l, list(enumerate(mine[:2])))
        rank(zz, [(o * CAP, d) for o, d in enumerate(mine[:2])]
             + [(own_slots + o * CAP, d) for o, d in enumerate(theirs[:2])])

    def stage_far(k):
        zz = source(side_len + k)
        for i in range(heads):
            recv_part(side_len + k, i, False)
        recv_meta(side_len + k, False)
        wy[...] = qb[0, zz]
        wym[...] = meta[0, zz]
        for m in range(ends):
            for cc in range(PAIR):
                es = [slot[(zz * 2 * finds + owners + m * PAIR + cc) * CAP + n] for n in range(CAP)]
                ym[k, m, cc] = jnp.concatenate([info(wym, es), jnp.zeros((1, wide), jnp.float32)], axis=0)
                for n in range(CAP):
                    x = lax.div(jnp.maximum(es[n], 0), sel)
                    ys[k, m, cc, n] = wy[lax.div(x, piece), :, lax.rem(x, piece)]
                for d in y_copy(k, m, cc):
                    d.start()

    def info(table, es):
        out = None
        for n in range(CAP):
            e = jnp.maximum(es[n], 0)
            m = table[lax.div(e, sel)]
            bits = jnp.zeros_like(m[0:1])
            for j in range(sel):
                bits = jnp.where((es[n] >= 0) & (lax.rem(e, sel) == j), m[2 + j:3 + j], bits)
            one = jnp.concatenate([m[0:2], bits], axis=0)
            out = one if n == 0 else jnp.where(lane < n * rows, out, one)
        return out

    @pl.when(is_gate)
    def _():
        @pl.loop(side_len, line)
        def _(t):
            zz = source(t)
            find(zz, 0, list(enumerate(mine + across)))
            find(zz, 1, list(enumerate(mine)))
            rank(zz, [(o * CAP, d) for o, d in enumerate(mine)]
                 + [(own_slots + o * CAP, d) for o, d in enumerate(theirs)]
                 + [(2 * own_slots + o * CAP, d) for o, d in enumerate(across)])
        stage_far(0)

    for a in range(heads):
        for o in range(2):
            if a or o:
                kv_from(other(a), o).wait_recv()
    for o in range(2):
        kt[o] = kv[o, :, 0].reshape(keys, width).astype(jnp.float32).T.astype(jnp.bfloat16)
    bit = lax.broadcasted_iota(jnp.int32, (cubes, 2 * wide), 0)

    def compute(o, qs, gs, both):
        kept = (both[2:3].astype(jnp.int32) >> bit) & 1
        lines = jnp.where(kept == 1, both[0:1], jnp.inf)
        kk = kv[o, :, 0].reshape(keys, width)
        vv = kv[o, :, 1].reshape(keys, width)
        st = lax.dot_general(kk, qs, NT, preferred_element_type=jnp.float32)
        dpt = lax.dot_general(vv, gs, NT, preferred_element_type=jnp.float32)
        st = st.reshape(cubes, rows, 2 * wide)
        p = jnp.exp2(st * (scale * LOG2E) - lines[:, None, :])
        ds = p * (dpt.reshape(cubes, rows, 2 * wide) - both[1:2][:, None, :])
        pb = p.astype(jnp.bfloat16).reshape(keys, 2 * wide)
        dsb = ds.astype(jnp.bfloat16).reshape(keys, 2 * wide)
        dv[o] += lax.dot_general(pb, gs, NN, preferred_element_type=jnp.float32)
        dk[o] += lax.dot_general(dsb, qs, NN, preferred_element_type=jnp.float32)
        dqt = lax.dot_general(kt[o], dsb, NN, preferred_element_type=jnp.float32)
        return (dqt.T * scale).astype(jnp.bfloat16).reshape(2, CAP, rows, width)

    def work(zz, o):
        es = [[slot[((zz * 2 + l) * finds + o) * CAP + k] for k in range(CAP)] for l in range(2)]
        xs = [(l, lax.div(jnp.maximum(e, 0), sel)) for l in range(2) for e in es[l]]
        qs = jnp.concatenate([wq[l, lax.div(x, piece), 0, lax.rem(x, piece)] for l, x in xs], axis=0)
        gs = jnp.concatenate([wq[l, lax.div(x, piece), 1, lax.rem(x, piece)] for l, x in xs], axis=0)
        both = jnp.concatenate([info(wm.at[0], es[0]), info(wm.at[1], es[1])], axis=1)
        dq = compute(o, qs, gs, both)
        own_dq[zz, o * CAP:(o + 1) * CAP] = dq[0]
        give[zz, o * CAP:(o + 1) * CAP] = dq[1]

    def works(t, many):
        zz = source(t)
        for p in range(heads):
            q_core(zz, p).wait_recv()
        m_core(zz).wait_recv()
        for l in range(2):
            wq[l] = qb[l, zz]
            wm[l] = meta[l, zz]
        for o in range(many):
            work(zz, o)
        give_copy(zz, many * CAP).start()

    def finish(t, many):
        zz = source(t)
        give_copy(zz, many * CAP).wait_recv()
        wr[0:many * CAP] = own_dq[zz, 0:many * CAP]
        wr[own_slots:own_slots + many * CAP] = got[zz, 0:many * CAP]
        if many > 2:
            k = t - side_len
            for m in range(ends):
                for cc in range(PAIR):
                    y_done(k, m, cc).wait_recv()
                    at = 2 * own_slots + (m * PAIR + cc) * CAP
                    wr[at:at + CAP] = yq[k, m, cc]
        for x in range(cubes):
            total = wr[ret_ix[(zz * cubes + x) * sel]].astype(jnp.float32)
            for j in range(1, sel):
                total = total + wr[ret_ix[(zz * cubes + x) * sel + j]].astype(jnp.float32)
            fin[zz, x // piece, x % piece] = total.astype(jnp.bfloat16)
        at = side_len if many > 2 else z - first
        for i in range(1, heads):
            fq_copy(i, zz, at).start()

        @pl.when(zz != z)
        def _():
            fq_copy(0, zz, at).start()

    def give_kv(o):
        for n, total in enumerate((dk[o] * scale, dv[o])):
            skv[o, :, n] = total.astype(jnp.bfloat16).reshape(heads, piece, rows, width)
        for t in range(heads):
            if t or o:
                fk_copy(t, o).start()

    keep_q = pltpu.make_async_copy(fin.at[z, h], retq_ref.at[z - first, h], loc_sem.at[1])
    keep_k = pltpu.make_async_copy(skv.at[0, h], retkv_ref.at[0, h], loc_sem.at[2])
    blank = pltpu.make_async_copy(skv.at[0], retkv_ref.at[2], loc_sem.at[3])

    @pl.when(is_gate)
    def _():
        skv[0] = jnp.zeros_like(skv[0])
        blank.start()

    @pl.loop(0, side_len)
    def _(t):
        works(t, 2)

    @pl.when(is_end)
    def _():
        give_kv(1)
        give_kv(0)

    @pl.when(is_gate)
    def _():
        for k in range(1, min(2, side_len)):
            stage_far(k)
        for m in range(ends):
            for a in range(heads):
                kv_from(a, 2 + m).wait_recv()
            kt[2 + m] = kv[2 + m, :, 0].reshape(keys, width).astype(jnp.float32).T.astype(jnp.bfloat16)

    @pl.loop(0, side_len)
    def _(t):
        finish(t, 2)

    @pl.when(is_gate)
    def _():
        @pl.loop(side_len, line)
        def _(t):
            k = t - side_len
            works(t, owners)
            for m in range(ends):
                for cc in range(PAIR):
                    for d in y_from(k, m, cc):
                        d.wait_recv()
                at = [(cc, n) for cc in range(PAIR) for n in range(CAP)]
                qs = jnp.concatenate([yr[k, m, cc, n, 0] for cc, n in at], axis=0)
                gs = jnp.concatenate([yr[k, m, cc, n, 1] for cc, n in at], axis=0)
                both = jnp.concatenate([yrm[k, m, cc] for cc in range(PAIR)], axis=1)
                dq = compute(2 + m, qs, gs, both)
                for cc in range(PAIR):
                    yd[k, m, cc] = dq[cc]
                    y_back(k, m, cc).start()

            @pl.when(k + 2 < side_len)
            def _():
                stage_far(k + 2)

        blank.wait()
        give_kv(1)
        for m in range(ends):
            give_kv(2 + m)
        give_kv(0)

        @pl.loop(side_len, line)
        def _(t):
            finish(t, owners)

    keep_q.start()
    keep_k.start()

    for m in range(1, side_len):
        for p in range(heads):
            q_own(p, m).wait_send()
        m_own(m).wait_send()
    for t in range(1, heads):
        q_cross(t).wait_send()
        d_cross(t).wait_send()
        kv_done(t, 0).wait_send()
    for t in range(heads):
        kv_done(t, 1).wait_send()
    for m in range(1, line):
        t_line(m).wait_send()
    t_core.wait_send()

    @pl.loop(0, side_len)
    def _(t):
        zz = source(t)
        for p in range(heads):
            q_core(zz, p).wait_send()
        m_core(zz).wait_send()
        give_copy(zz, 2 * CAP).wait_send()

    @pl.when(is_end)
    def _():
        for t in range(heads):
            kv_done(t, 2).wait_send()
            fk_from(other(t), 2).wait_recv()

    @pl.when(is_gate)
    def _():
        for p in range(heads):
            q_own(p, 0).wait_send()
        m_own(0).wait_send()
        for t in range(1, side_len):
            for p in range(heads):
                q_relay(near(t), p).wait_send()
            m_relay(near(t)).wait_send()
        for t in range(side_len, line):
            k = t - side_len
            zz = source(t)
            for p in range(heads):
                q_core(zz, p).wait_send()
            m_core(zz).wait_send()
            give_copy(zz, owners * CAP).wait_send()
            for m in range(ends):
                for cc in range(PAIR):
                    for d in y_copy(k, m, cc):
                        d.wait_send()
                    y_back(k, m, cc).wait_send()
            for i in range(heads):
                fq_copy(i, zz, side_len).wait_send()
        for m in range(ends):
            for t in range(heads):
                fk_copy(t, 2 + m).wait_send()

    for t in range(heads):
        for o in range(2):
            if t or o:
                fk_copy(t, o).wait_send()
                fk_from(other(t), o).wait_recv()
        for m in range(side_len):
            if t or m:
                zz = near(m)
                fq_copy(t, zz, z - first).wait_send()
                fq_from(zz - first, other(t)).wait_recv()
        fq_from(side_len, other(t)).wait_recv()
    keep_q.wait()
    keep_k.wait()


def place(q_ref, kv_ref, oq_ref, ok_ref, ov_ref):
    line, heads, piece, rows, width = q_ref.shape
    for a in range(heads):
        at = slice(a * width, (a + 1) * width)
        total = q_ref[0, a].astype(jnp.float32)
        for m in range(1, line):
            total = total + q_ref[m, a].astype(jnp.float32)
        oq_ref[:, :, at] = total.astype(jnp.bfloat16)
        for n, out in enumerate((ok_ref, ov_ref)):
            total = kv_ref[0, a, n].astype(jnp.float32)
            for m in range(1, kv_ref.shape[0]):
                total = total + kv_ref[m, a, n].astype(jnp.float32)
            out[:, :, at] = total.astype(jnp.bfloat16)


def on_device(
    query_rows, key_rows, value_rows, output_grad, output_rows, row_logsumexp,
    chosen_owner, chosen_cubes,
):
    heads = lax.axis_size("head")
    seqs = lax.axis_size("seq")
    piece_rows, full = query_rows.shape[2:]
    width = full // heads
    cubes, sel = chosen_owner.shape
    tokens = row_logsumexp.shape[0]
    rows = tokens // cubes
    piece = piece_rows // rows
    wide = CAP * rows
    line = seqs // (PAIR * SHARE)
    side_len = line // 2
    keys = cubes * rows
    metas = 2 + sel

    def cubed(a):
        return a.reshape(piece, rows, full)

    bf, f32, i32 = jnp.bfloat16, jnp.float32, jnp.int32
    vmem = pl.BlockSpec(memory_space=pltpu.VMEM)
    anywhere = pl.BlockSpec(memory_space=pl.ANY)
    smem = pl.BlockSpec(memory_space=pltpu.SMEM)
    dma = pltpu.SemaphoreType.DMA
    ends = side_len - 1
    owners = 2 + ends
    slots = owners * CAP
    finds = owners + PAIR * ends
    unit = (heads, 2, piece, rows, width)
    pair = (side_len, ends, PAIR)
    outs = pl.pallas_call(
        functools.partial(kernel, heads, seqs, sel),
        out_shape=[
            jax.ShapeDtypeStruct((side_len + 1, heads, piece, rows, width), bf),
            jax.ShapeDtypeStruct((3, *unit), bf),
        ],
        in_specs=[smem, vmem] + [anywhere] * 5 + [vmem],
        out_specs=[anywhere] * 2,
        scratch_shapes=[
            pltpu.VMEM((2, line, *unit), bf),
            pltpu.VMEM((owners, *unit), bf),
            pltpu.VMEM((owners, width, keys), bf),
            pltpu.VMEM((piece, rows, full), bf),
            pltpu.VMEM((piece, rows, full), bf),
            pltpu.VMEM((heads, piece, metas, wide), f32),
            pltpu.VMEM((cubes, metas, wide), f32),
            pltpu.VMEM((cubes, metas, wide), f32),
            pltpu.VMEM((2, line, cubes, metas, wide), f32),
            pltpu.VMEM((2, line, sel, cubes), i32),
            pltpu.SMEM((2, line, sel, cubes), i32),
            pltpu.SMEM((line * 2 * finds * CAP,), i32),
            pltpu.SMEM((line * cubes * sel,), i32),
            pltpu.VMEM((2, *unit), bf),
            pltpu.VMEM((2, cubes, metas, wide), f32),
            pltpu.VMEM(unit, bf),
            pltpu.VMEM((cubes, metas, wide), f32),
            pltpu.VMEM((owners, keys, width), f32),
            pltpu.VMEM((owners, keys, width), f32),
            pltpu.VMEM((line, slots, rows, width), bf),
            pltpu.VMEM((line, slots, rows, width), bf),
            pltpu.VMEM((line, slots, rows, width), bf),
            pltpu.VMEM((2 * slots + 2 * ends * CAP + 1, rows, width), bf),
            pltpu.VMEM((line, heads, piece, rows, width), bf),
            pltpu.VMEM((owners, *unit), bf),
            pltpu.VMEM((*pair, CAP, 2, rows, width), bf),
            pltpu.VMEM((*pair, 4, wide), f32),
            pltpu.VMEM((*pair, CAP, 2, rows, width), bf),
            pltpu.VMEM((*pair, 4, wide), f32),
            pltpu.VMEM((*pair, CAP, rows, width), bf),
            pltpu.VMEM((*pair, CAP, rows, width), bf),
            dma((6,)),
            dma((heads,)), dma((heads, side_len)), dma((line, heads)), dma((line, heads)),
            dma((line, heads)), dma((line, heads)),
            dma((side_len,)), dma((line,)), dma((line,)), dma((line,)), dma((line,)),
            dma((line,)), dma((line,)), dma((1,)), dma((1,)),
            dma((heads,)), dma((heads,)),
            dma((heads, 3)), dma((owners, heads)),
            dma((line,)), dma((line,)),
            dma((line, heads)), dma((side_len + 1, heads)), dma((owners, heads)), dma((3, heads)),
            dma(pair), dma(pair), dma(pair), dma(pair), dma(pair), dma(pair),
        ],
        compiler_params=pltpu.CompilerParams(
            collective_id=0, has_side_effects=True),
    )(
        chosen_cubes, chosen_owner.T, cubed(query_rows), cubed(key_rows), cubed(value_rows),
        cubed(output_grad), cubed(output_rows),
        row_logsumexp.reshape(1, tokens),
    )
    outs = pl.pallas_call(
        place,
        out_shape=[jax.ShapeDtypeStruct((piece, rows, full), bf)] * 3,
        in_specs=[vmem] * 2,
        out_specs=[vmem] * 3,
    )(*outs)
    return tuple(a.reshape(1, 1, piece_rows, full) for a in outs)


def solution(mesh):
    rows = P("seq", "head", None, None)
    return jax.shard_map(
        on_device,
        mesh=mesh,
        in_specs=(rows, rows, rows, rows, rows, P("seq", "head"), P("seq", None), P("seq", None, None)),
        out_specs=(rows, rows, rows),
        check_vma=False,
    )
```

```python
import functools
import math

import jax
import jax.numpy as jnp
from jax import lax
from jax.experimental import pallas as pl
from jax.experimental.pallas import tpu as pltpu
from jax.sharding import PartitionSpec as P

CAP = 2
PAIR = 2
SHARE = 2
LOG2E = math.log2(math.e)
NT = (((1,), (1,)), ((), ()))
NN = (((1,), (0,)), ((), ()))


def kernel(
    heads, seqs, sel,
    pick_ref, table_ref, q_ref, k_ref, v_ref, g_ref, o_ref, lse_ref,
    retq_ref, retkv_ref,
    qb, kv, kt, g_all, o_all, dsend, dlt, base, meta, tab, tab_s,
    slot, ret_ix, wq, wm, wy, wym, dk, dv, own_dq, give, got, wr, fin, skv,
    ys, ym, yr, yrm, yd, yq, part,
    loc_sem, qx_s, qn_s, qg_s, q_r, qc_s, qc_r, mn_s, mg_s, m_r, mc_s, mc_r,
    t_s, t_r, tc_s, tc_r, dl_s, dl_r, kv_s, kv_r, gv_s, gv_r, fq_s, fq_r, fk_s, fk_r,
    ys_s, ys_r, ym_s, ym_r, yd_s, yd_r, part_r,
):
    h = lax.axis_index("head")
    s = lax.axis_index("seq")
    group = PAIR * SHARE
    line = seqs // group
    z = s // group
    y = (s // PAIR) % SHARE
    c = s % PAIR
    side_len = line // 2
    ends = side_len - 1
    side = z // side_len
    first = side * side_len
    _, _, _, _, piece, rows, width = qb.shape
    cubes = heads * piece
    keys = cubes * rows
    wide = CAP * rows
    metas = meta.shape[3]
    scale = 1.0 / math.sqrt(width)
    gate_here = (1 - side) * (side_len - 1) + side * side_len
    gate_far = (1 - side) * side_len + side * (side_len - 1)
    is_gate = z == gate_here
    is_end = z != gate_here
    owners = 2 + ends
    finds = owners + 2 * ends
    own_slots = owners * CAP
    zero_slot = 2 * own_slots + 2 * ends * CAP

    def dev(hh, zz, yy, cc):
        return {"head": hh, "seq": zz * group + yy * PAIR + cc}

    def near(t):
        return first + (z - first + t) % side_len

    def source(t):
        is_far = t // side_len
        k = t - side_len
        far = (1 - side) * (side_len + k) + side * (side_len - 1 - k)
        return (1 - is_far) * near(t) + is_far * far

    def other(t):
        return (h + t) % heads

    barrier = pltpu.get_barrier_semaphore()
    for t in range(heads):
        pl.semaphore_signal(barrier, inc=1, device_id=dev(other(t), z, 1 - y, c))
        for m in range(line):
            if t or m:
                pl.semaphore_signal(barrier, inc=1, device_id=dev(other(t), (z + m) % line, y, c))
    pl.semaphore_signal(barrier, inc=1, device_id=dev(h, z, y, 1 - c))
    pl.semaphore_signal(barrier, inc=1, device_id=dev(h, z, 1 - y, 1 - c))
    partners = heads + heads * line + 1

    def cols(a):
        return pl.ds(pl.multiple_of(a * width, width), width)

    def rows_of(a):
        return pl.ds(a * piece, piece)

    loads = [pltpu.make_async_copy(g_ref, g_all, loc_sem.at[0]),
             pltpu.make_async_copy(o_ref, o_all, loc_sem.at[1])]
    stage = []
    for n, (a, b) in enumerate(((q_ref, k_ref), (g_ref, v_ref))):
        stage.append(pltpu.make_async_copy(a.at[:, :, cols(h)], qb.at[0, z, h, n], loc_sem.at[2 + n]))
        stage.append(pltpu.make_async_copy(b.at[:, :, cols(h)], kv.at[0, h, n], loc_sem.at[4 + n]))
    for d in loads + stage:
        d.start()

    pl.semaphore_wait(barrier, partners)

    def remote(src, dst, send, recv, to):
        return pltpu.make_async_remote_copy(
            src_ref=src, dst_ref=dst, send_sem=send, recv_sem=recv, device_id=to)

    def hop(m):
        return gate_far if m == 0 else near(m)

    def q_own(p, m, n):
        return remote(qb.at[0, z, p, n], qb.at[0, z, p, n], qn_s.at[p, m, n], q_r.at[z, p, n], dev(h, hop(m), y, c))

    def q_relay(zz, p, n):
        return remote(qb.at[0, zz, p, n], qb.at[0, zz, p, n], qg_s.at[zz, p, n], q_r.at[zz, p, n],
                      dev(h, gate_far, y, c))

    def q_cross(t, n):
        a = other(t)
        return remote(qb.at[0, z, a, n], qb.at[0, z, h, n], qx_s.at[t, n], q_r.at[z, h, n], dev(a, z, y, c))

    def q_core(zz, p, n):
        return remote(qb.at[0, zz, p, n], qb.at[1, zz, p, n], qc_s.at[zz, p, n], qc_r.at[zz, p, n],
                      dev(h, z, y, 1 - c))

    def m_own(m):
        return remote(meta.at[0, z], meta.at[0, z], mn_s.at[m], m_r.at[z], dev(h, hop(m), y, c))

    def m_relay(zz):
        return remote(meta.at[0, zz], meta.at[0, zz], mg_s.at[zz], m_r.at[zz], dev(h, gate_far, y, c))

    def m_core(zz):
        return remote(meta.at[0, zz], meta.at[1, zz], mc_s.at[zz], mc_r.at[zz], dev(h, z, y, 1 - c))

    def t_line(m):
        return remote(table_ref, tab.at[0, z], t_s.at[m], t_r.at[z], dev(h, (z + m) % line, y, c))

    def t_from(zz):
        return remote(table_ref, tab.at[0, zz], t_s.at[0], t_r.at[zz], dev(h, zz, y, c))

    t_core = remote(tab.at[0], tab.at[1], tc_s.at[0], tc_r.at[0], dev(h, z, y, 1 - c))

    def d_cross(t):
        a = other(t)
        return remote(dsend.at[a], dlt.at[rows_of(h)], dl_s.at[t], dl_r.at[h], dev(a, z, y, c))

    def d_from(a):
        return remote(dsend.at[a], dlt.at[rows_of(a)], dl_s.at[0], dl_r.at[a], dev(a, z, y, c))

    def kv_done(t, o):
        return remote(kv.at[0, h], kv.at[o, h], kv_s.at[t, o], kv_r.at[o, h], dev(other(t), z, 1 - y, c))

    def kv_from(a, o):
        return remote(kv.at[0, h], kv.at[o, a], kv_s.at[0, 0], kv_r.at[o, a], dev(h, z, 1 - y, c))

    def give_copy(zz, count):
        part = pl.ds(0, count)
        return remote(give.at[zz, part], got.at[zz, part], gv_s.at[zz], gv_r.at[zz], dev(h, z, y, 1 - c))

    def fq_copy(t, zz, at):
        a = other(t)
        return remote(fin.at[zz, a], retq_ref.at[at, h], fq_s.at[zz, t], fq_r.at[at, h], dev(a, zz, y, c))

    def fq_from(at, a):
        return remote(fin.at[z, a], retq_ref.at[at, a], fq_s.at[0, 0], fq_r.at[at, a], dev(a, gate_far, y, c))

    def fk_copy(t, o):
        a = other(t)
        to, kind = (dev(h, z, 1 - y, c), 0) if o == 1 else (dev(h, near(o - 1), y, c), 1)
        return remote(skv.at[o, a], part.at[kind, a], fk_s.at[o, t], part_r.at[kind, a], to)

    def fk_from(a, kind):
        return remote(skv.at[0, a], part.at[kind, a], fk_s.at[0, 0], part_r.at[kind, a], dev(h, z, 1 - y, c))

    def fk_cross(t):
        a = other(t)
        return remote(skv.at[0, a], retkv_ref.at[h], fk_s.at[0, t], fk_r.at[h], dev(a, z, y, c))

    def fk_done(a):
        return remote(skv.at[0, a], retkv_ref.at[a], fk_s.at[0, 0], fk_r.at[a], dev(a, z, y, c))

    def y_copy(k, m, cc):
        return (
            remote(ys.at[k, m, cc], yr.at[k, m, c], ys_s.at[k, m, cc], ys_r.at[k, m, c], dev(h, z, 1 - y, cc)),
            remote(ym.at[k, m, cc], yrm.at[k, m, c], ym_s.at[k, m, cc], ym_r.at[k, m, c], dev(h, z, 1 - y, cc)),
        )

    def y_from(k, m, cc):
        return (
            remote(ys.at[k, m, cc], yr.at[k, m, cc], ys_s.at[k, m, cc], ys_r.at[k, m, cc], dev(h, z, 1 - y, cc)),
            remote(ym.at[k, m, cc], yrm.at[k, m, cc], ym_s.at[k, m, cc], ym_r.at[k, m, cc], dev(h, z, 1 - y, cc)),
        )

    def y_back(k, m, cc):
        return remote(yd.at[k, m, cc], yq.at[k, m, c], yd_s.at[k, m, cc], yd_r.at[k, m, c], dev(h, z, 1 - y, cc))

    def y_done(k, m, cc):
        return remote(yd.at[k, m, cc], yq.at[k, m, cc], yd_s.at[k, m, cc], yd_r.at[k, m, cc], dev(h, z, 1 - y, cc))

    def send_parts(srcs, dst, send, recv, a, to):
        for n, src in enumerate(srcs):
            remote(src.at[:, :, cols(a)], dst.at[n], send, recv, to).start()

    def send_q(dst, send, recv, a, to):
        for n, src in enumerate((q_ref, g_ref)):
            remote(src.at[:, :, cols(a)], dst.at[n], send.at[n], recv.at[n], to).start()

    def first_part(m):
        send_q(qb.at[0, z, h], qn_s.at[h, m], q_r.at[z, h], h, dev(h, hop(m), y, c))

    for m in range(1, line):
        t_line(m).start()

    @pl.when(is_gate)
    def _():
        first_part(0)

    for m in range(1, side_len):
        first_part(m)
    for t in range(1, heads):
        send_q(qb.at[0, z, h], qx_s.at[t], q_r.at[z, h], other(t), dev(other(t), z, y, c))
    send_q(qb.at[1, z, h], qc_s.at[z, h], qc_r.at[z, h], h, dev(h, z, y, 1 - c))

    row = lax.broadcasted_iota(jnp.int32, (metas, wide), 0)
    lane = lax.broadcasted_iota(jnp.int32, (3, wide), 1)
    for d in loads:
        d.wait()
    for a in range(heads):
        for x in range(piece):
            prod = g_all[x, :, a * width:(a + 1) * width].astype(jnp.float32) * o_all[
                x, :, a * width:(a + 1) * width
            ].astype(jnp.float32)
            both = jnp.concatenate([prod] * CAP, axis=0)
            total = jnp.sum(both.T, axis=0, keepdims=True)
            dsend[a, x] = jnp.where(row == 1, jnp.broadcast_to(total, (metas, wide)), 0.0)
    for t in range(1, heads):
        d_cross(t).start()
    for t in range(heads):
        for o in (1, 0):
            if t or o:
                send_parts((k_ref, v_ref), kv.at[o, h], kv_s.at[t, o], kv_r.at[o, h], other(t),
                           dev(other(t), z, (y + o) % SHARE, c))

    for x in range(cubes):
        line_x = jnp.concatenate([lse_ref[:, x * rows:(x + 1) * rows] * LOG2E] * CAP, axis=1)
        both = jnp.where(row == 0, jnp.broadcast_to(line_x, (metas, wide)), 0.0)
        for j in range(sel):
            bits = jnp.int32(0)
            for k in range(cubes):
                bits = bits + jnp.where(pick_ref[x, j, k] != 0, 1 << k, 0)
            both = jnp.where(row == 2 + j, bits.astype(jnp.float32), both)
        base[x] = both
    tab[0, z] = table_ref[...]
    dlt[rows_of(h)] = dsend[h]
    for d in stage:
        d.wait()

    def recv_part(t, i, relays):
        zz = source(t)
        p = other(i)
        for n in range(2):
            q_relay(zz, p, n).wait_recv()
            if relays:
                q_relay(zz, p, n).start()
            q_core(zz, p, n).start()

    def recv_meta(t, relays):
        zz = source(t)
        m_relay(zz).wait_recv()
        if relays:
            m_relay(zz).start()
        m_core(zz).start()

    for t in range(1, heads):
        for n in range(2):
            q_relay(z, other(t), n).wait_recv()

            @pl.when(is_gate)
            def _():
                q_own(other(t), 0, n).start()

            for m in range(1, side_len):
                q_own(other(t), m, n).start()
            q_core(z, other(t), n).start()

    @pl.when(is_gate)
    def _():
        for t in range(1, side_len):
            recv_part(t, 0, True)

    for t in range(1, heads):
        d_from(other(t)).wait_recv()
    for x in range(cubes):
        meta[0, z, x] = base[x] + dlt[x]

    @pl.when(is_gate)
    def _():
        m_own(0).start()

    for m in range(1, side_len):
        m_own(m).start()
    m_core(z).start()

    @pl.when(is_end)
    def _():
        at = 1 + (z - gate_here + side_len) % side_len
        for t in range(heads):
            send_parts((k_ref, v_ref), kv.at[at, h], kv_s.at[t, 2], kv_r.at[at, h], other(t),
                       dev(other(t), gate_here, y, c))

    dk[...] = jnp.zeros_like(dk)
    dv[...] = jnp.zeros_like(dv)
    wr[zero_slot] = jnp.zeros_like(wr[zero_slot])

    for m in range(1, line):
        t_from((z + m) % line).wait_recv()
    t_core.start()

    t_core.wait_recv()
    to_smem = pltpu.make_async_copy(tab, tab_s, loc_sem.at[0])
    to_smem.start()
    to_smem.wait()

    def number(zz, yy, cc):
        return zz * group + yy * PAIR + cc

    mine = [number(z, y, c), number(z, 1 - y, c)]
    mine = mine + [number(near(m), y, c) for m in range(1, side_len)]
    across = [number(near(m), 1 - y, cc) for m in range(1, side_len) for cc in range(PAIR)]
    theirs = [number(z, y, 1 - c), number(z, 1 - y, 1 - c)]
    theirs = theirs + [number(near(m), y, 1 - c) for m in range(1, side_len)]

    def find(zz, l, who):
        for o, d in who:
            found = [jnp.int32(-1)] * CAP
            for e in range(cubes * sel - 1, -1, -1):
                hit = tab_s[l, zz, e % sel, e // sel] == d
                for k in range(CAP - 1, 0, -1):
                    found[k] = jnp.where(hit, found[k - 1], found[k])
                found[0] = jnp.where(hit, e, found[0])
            for k in range(CAP):
                slot[((zz * 2 + l) * finds + o) * CAP + k] = found[k]

    def rank(zz, who):
        count = [jnp.int32(0)] * len(who)
        for e in range(cubes * sel):
            d = tab_s[0, zz, e % sel, e // sel]
            ix = jnp.int32(zero_slot)
            for n, (at, d_n) in enumerate(who):
                hit = d == d_n
                ix = jnp.where(hit, at + jnp.minimum(count[n], CAP - 1), ix)
                count[n] = count[n] + hit.astype(jnp.int32)
            ret_ix[zz * cubes * sel + e] = ix

    @pl.loop(0, side_len)
    def _(t):
        zz = source(t)
        for l in range(2):
            find(zz, l, list(enumerate(mine[:2])))
        rank(zz, [(o * CAP, d) for o, d in enumerate(mine[:2])]
             + [(own_slots + o * CAP, d) for o, d in enumerate(theirs[:2])])

    @pl.when(is_gate)
    def _():
        @pl.loop(side_len, line)
        def _(t):
            zz = source(t)
            find(zz, 0, list(enumerate(mine + across)))
            find(zz, 1, list(enumerate(mine)))
            rank(zz, [(o * CAP, d) for o, d in enumerate(mine)]
                 + [(own_slots + o * CAP, d) for o, d in enumerate(theirs)]
                 + [(2 * own_slots + o * CAP, d) for o, d in enumerate(across)])

    @pl.when(is_gate)
    def _():
        for t in range(1, side_len):
            for i in range(1, heads):
                recv_part(t, i, True)
            recv_meta(t, True)

    @pl.when(is_end)
    def _():
        for t in range(1, side_len):
            for i in range(heads):
                recv_part(t, i, False)
            recv_meta(t, False)

    def stage_far(k):
        zz = source(side_len + k)
        for i in range(heads):
            recv_part(side_len + k, i, False)
        recv_meta(side_len + k, False)
        wy[...] = qb[0, zz]
        wym[...] = meta[0, zz]
        for m in range(ends):
            for cc in range(PAIR):
                es = [slot[(zz * 2 * finds + owners + m * PAIR + cc) * CAP + n] for n in range(CAP)]
                ym[k, m, cc] = jnp.concatenate([info(wym, es), jnp.zeros((1, wide), jnp.float32)], axis=0)
                for n in range(CAP):
                    x = lax.div(jnp.maximum(es[n], 0), sel)
                    ys[k, m, cc, n] = wy[lax.div(x, piece), :, lax.rem(x, piece)]
                for d in y_copy(k, m, cc):
                    d.start()

    def info(table, es):
        out = None
        for n in range(CAP):
            e = jnp.maximum(es[n], 0)
            m = table[lax.div(e, sel)]
            bits = jnp.zeros_like(m[0:1])
            for j in range(sel):
                bits = jnp.where((es[n] >= 0) & (lax.rem(e, sel) == j), m[2 + j:3 + j], bits)
            one = jnp.concatenate([m[0:2], bits], axis=0)
            out = one if n == 0 else jnp.where(lane < n * rows, out, one)
        return out

    @pl.when(is_gate)
    def _():
        stage_far(0)

    for a in range(heads):
        for o in range(2):
            if a or o:
                kv_from(other(a), o).wait_recv()
    for o in range(2):
        kt[o] = kv[o, :, 0].reshape(keys, width).astype(jnp.float32).T.astype(jnp.bfloat16)
    bit = lax.broadcasted_iota(jnp.int32, (cubes, 2 * wide), 0)

    def compute(o, qs, gs, both):
        kept = (both[2:3].astype(jnp.int32) >> bit) & 1
        lines = jnp.where(kept == 1, both[0:1], jnp.inf)
        kk = kv[o, :, 0].reshape(keys, width)
        vv = kv[o, :, 1].reshape(keys, width)
        st = lax.dot_general(kk, qs, NT, preferred_element_type=jnp.float32)
        dpt = lax.dot_general(vv, gs, NT, preferred_element_type=jnp.float32)
        st = st.reshape(cubes, rows, 2 * wide)
        p = jnp.exp2(st * (scale * LOG2E) - lines[:, None, :])
        ds = p * (dpt.reshape(cubes, rows, 2 * wide) - both[1:2][:, None, :])
        pb = p.astype(jnp.bfloat16).reshape(keys, 2 * wide)
        dsb = ds.astype(jnp.bfloat16).reshape(keys, 2 * wide)
        dv[o] += lax.dot_general(pb, gs, NN, preferred_element_type=jnp.float32)
        dk[o] += lax.dot_general(dsb, qs, NN, preferred_element_type=jnp.float32)
        dqt = lax.dot_general(kt[o], dsb, NN, preferred_element_type=jnp.float32)
        return (dqt.T * scale).astype(jnp.bfloat16).reshape(2, CAP, rows, width)

    def work(zz, o):
        es = [[slot[((zz * 2 + l) * finds + o) * CAP + k] for k in range(CAP)] for l in range(2)]
        xs = [(l, lax.div(jnp.maximum(e, 0), sel)) for l in range(2) for e in es[l]]
        qs = jnp.concatenate([wq[l, lax.div(x, piece), 0, lax.rem(x, piece)] for l, x in xs], axis=0)
        gs = jnp.concatenate([wq[l, lax.div(x, piece), 1, lax.rem(x, piece)] for l, x in xs], axis=0)
        both = jnp.concatenate([info(wm.at[0], es[0]), info(wm.at[1], es[1])], axis=1)
        dq = compute(o, qs, gs, both)
        own_dq[zz, o * CAP:(o + 1) * CAP] = dq[0]
        give[zz, o * CAP:(o + 1) * CAP] = dq[1]

    def works(t, many):
        zz = source(t)
        for p in range(heads):
            for n in range(2):
                q_core(zz, p, n).wait_recv()
        m_core(zz).wait_recv()
        for l in range(2):
            wq[l] = qb[l, zz]
            wm[l] = meta[l, zz]
        for o in range(many):
            work(zz, o)
        give_copy(zz, many * CAP).start()

    def finish(t, many):
        zz = source(t)
        give_copy(zz, many * CAP).wait_recv()
        wr[0:many * CAP] = own_dq[zz, 0:many * CAP]
        wr[own_slots:own_slots + many * CAP] = got[zz, 0:many * CAP]
        if many > 2:
            k = t - side_len
            for m in range(ends):
                for cc in range(PAIR):
                    y_done(k, m, cc).wait_recv()
                    at = 2 * own_slots + (m * PAIR + cc) * CAP
                    wr[at:at + CAP] = yq[k, m, cc]
        for x in range(cubes):
            total = wr[ret_ix[(zz * cubes + x) * sel]].astype(jnp.float32)
            for j in range(1, sel):
                total = total + wr[ret_ix[(zz * cubes + x) * sel + j]].astype(jnp.float32)
            fin[zz, x // piece, x % piece] = total.astype(jnp.bfloat16)
        at = side_len if many > 2 else z - first
        for i in range(1, heads):
            fq_copy(i, zz, at).start()

        @pl.when(zz != z)
        def _():
            fq_copy(0, zz, at).start()

    def span(a):
        return pl.ds(pl.multiple_of(a * piece * rows, piece * rows), piece * rows)

    def give_part(t, o):
        a = other(t)
        for n, total in enumerate((dk[o, span(a)] * scale, dv[o, span(a)])):
            skv[o, a, n] = total.astype(jnp.bfloat16).reshape(piece, rows, width)
        fk_copy(t, o).start()

    def total_part(t, kinds):
        a = other(t)
        for kind in range(kinds):
            fk_from(a, kind).wait_recv()
        for n, total in enumerate((dk[0, span(a)] * scale, dv[0, span(a)])):
            total = total.reshape(piece, rows, width)
            for kind in range(kinds):
                total = total + part[kind, a, n].astype(jnp.float32)
            skv[0, a, n] = total.astype(jnp.bfloat16)
        if t:
            fk_cross(t).start()
        else:
            keep_k.start()

    later = list(range(1, heads))
    keep_q = pltpu.make_async_copy(fin.at[z, h], retq_ref.at[z - first, h], loc_sem.at[1])
    keep_k = pltpu.make_async_copy(skv.at[0, h], retkv_ref.at[h], loc_sem.at[2])

    @pl.loop(0, side_len)
    def _(t):
        works(t, 2)

    @pl.when(is_end)
    def _():
        for t in later + [0]:
            give_part(t, 1)

    @pl.when(is_gate)
    def _():
        for k in range(1, min(2, side_len)):
            stage_far(k)
        for m in range(ends):
            for a in range(heads):
                kv_from(a, 2 + m).wait_recv()
            kt[2 + m] = kv[2 + m, :, 0].reshape(keys, width).astype(jnp.float32).T.astype(jnp.bfloat16)

    @pl.loop(0, side_len)
    def _(t):
        finish(t, 2)

    keep_q.start()

    @pl.when(is_end)
    def _():
        for t in later + [0]:
            total_part(t, 2)

    @pl.when(is_gate)
    def _():
        def across_work(t):
            k = t - side_len
            for m in range(ends):
                for cc in range(PAIR):
                    for d in y_from(k, m, cc):
                        d.wait_recv()
                at = [(cc, n) for cc in range(PAIR) for n in range(CAP)]
                qs = jnp.concatenate([yr[k, m, cc, n, 0] for cc, n in at], axis=0)
                gs = jnp.concatenate([yr[k, m, cc, n, 1] for cc, n in at], axis=0)
                both = jnp.concatenate([yrm[k, m, cc] for cc in range(PAIR)], axis=1)
                dq = compute(2 + m, qs, gs, both)
                for cc in range(PAIR):
                    yd[k, m, cc] = dq[cc]
                    y_back(k, m, cc).start()

        @pl.loop(side_len, line)
        def _(t):
            works(t, owners)

            @pl.when(t + 2 < line)
            def _():
                stage_far(t + 2 - side_len)

            across_work(t)

            @pl.when((t > side_len) & (t + 1 < line))
            def _():
                finish(t - 1, owners)

        for m in range(ends):
            for t in later + [0]:
                give_part(t, 2 + m)
        for t in later + [0]:
            give_part(t, 1)
        finish(line - 2, owners)
        finish(line - 1, owners)
        for t in later + [0]:
            total_part(t, 1)

    for m in range(1, side_len):
        for p in range(heads):
            for n in range(2):
                q_own(p, m, n).wait_send()
        m_own(m).wait_send()
    for t in range(1, heads):
        for n in range(2):
            q_cross(t, n).wait_send()
        d_cross(t).wait_send()
        kv_done(t, 0).wait_send()
    for t in range(heads):
        kv_done(t, 1).wait_send()
    for m in range(1, line):
        t_line(m).wait_send()
    t_core.wait_send()

    @pl.loop(0, side_len)
    def _(t):
        zz = source(t)
        for p in range(heads):
            for n in range(2):
                q_core(zz, p, n).wait_send()
        m_core(zz).wait_send()
        give_copy(zz, 2 * CAP).wait_send()

    @pl.when(is_end)
    def _():
        for t in range(heads):
            kv_done(t, 2).wait_send()

    @pl.when(is_gate)
    def _():
        for p in range(heads):
            for n in range(2):
                q_own(p, 0, n).wait_send()
        m_own(0).wait_send()
        for t in range(1, side_len):
            for p in range(heads):
                for n in range(2):
                    q_relay(near(t), p, n).wait_send()
            m_relay(near(t)).wait_send()
        for t in range(side_len, line):
            k = t - side_len
            zz = source(t)
            for p in range(heads):
                for n in range(2):
                    q_core(zz, p, n).wait_send()
            m_core(zz).wait_send()
            give_copy(zz, owners * CAP).wait_send()
            for m in range(ends):
                for cc in range(PAIR):
                    for d in y_copy(k, m, cc):
                        d.wait_send()
                    y_back(k, m, cc).wait_send()
            for i in range(heads):
                fq_copy(i, zz, side_len).wait_send()
        for m in range(ends):
            for t in range(heads):
                fk_copy(t, 2 + m).wait_send()

    for t in range(heads):
        fk_copy(t, 1).wait_send()
        if t:
            fk_cross(t).wait_send()
            fk_done(other(t)).wait_recv()
        for m in range(side_len):
            if t or m:
                zz = near(m)
                fq_copy(t, zz, z - first).wait_send()
                fq_from(zz - first, other(t)).wait_recv()
        fq_from(side_len, other(t)).wait_recv()
    keep_q.wait()
    keep_k.wait()


def place(q_ref, kv_ref, oq_ref, ok_ref, ov_ref):
    line, heads, piece, rows, width = q_ref.shape
    for a in range(heads):
        at = slice(a * width, (a + 1) * width)
        total = q_ref[0, a].astype(jnp.float32)
        for m in range(1, line):
            total = total + q_ref[m, a].astype(jnp.float32)
        oq_ref[:, :, at] = total.astype(jnp.bfloat16)
        for n, out in enumerate((ok_ref, ov_ref)):
            out[:, :, at] = kv_ref[a, n]


def on_device(
    query_rows, key_rows, value_rows, output_grad, output_rows, row_logsumexp,
    chosen_owner, chosen_cubes,
):
    heads = lax.axis_size("head")
    seqs = lax.axis_size("seq")
    piece_rows, full = query_rows.shape[2:]
    width = full // heads
    cubes, sel = chosen_owner.shape
    tokens = row_logsumexp.shape[0]
    rows = tokens // cubes
    piece = piece_rows // rows
    wide = CAP * rows
    line = seqs // (PAIR * SHARE)
    side_len = line // 2
    keys = cubes * rows
    metas = 2 + sel

    def cubed(a):
        return a.reshape(piece, rows, full)

    bf, f32, i32 = jnp.bfloat16, jnp.float32, jnp.int32
    vmem = pl.BlockSpec(memory_space=pltpu.VMEM)
    anywhere = pl.BlockSpec(memory_space=pl.ANY)
    smem = pl.BlockSpec(memory_space=pltpu.SMEM)
    dma = pltpu.SemaphoreType.DMA
    ends = side_len - 1
    owners = 2 + ends
    slots = owners * CAP
    finds = owners + PAIR * ends
    unit = (heads, 2, piece, rows, width)
    pair = (side_len, ends, PAIR)
    outs = pl.pallas_call(
        functools.partial(kernel, heads, seqs, sel),
        out_shape=[
            jax.ShapeDtypeStruct((side_len + 1, heads, piece, rows, width), bf),
            jax.ShapeDtypeStruct(unit, bf),
        ],
        in_specs=[smem, vmem] + [anywhere] * 5 + [vmem],
        out_specs=[anywhere] * 2,
        scratch_shapes=[
            pltpu.VMEM((2, line, *unit), bf),
            pltpu.VMEM((owners, *unit), bf),
            pltpu.VMEM((owners, width, keys), bf),
            pltpu.VMEM((piece, rows, full), bf),
            pltpu.VMEM((piece, rows, full), bf),
            pltpu.VMEM((heads, piece, metas, wide), f32),
            pltpu.VMEM((cubes, metas, wide), f32),
            pltpu.VMEM((cubes, metas, wide), f32),
            pltpu.VMEM((2, line, cubes, metas, wide), f32),
            pltpu.VMEM((2, line, sel, cubes), i32),
            pltpu.SMEM((2, line, sel, cubes), i32),
            pltpu.SMEM((line * 2 * finds * CAP,), i32),
            pltpu.SMEM((line * cubes * sel,), i32),
            pltpu.VMEM((2, *unit), bf),
            pltpu.VMEM((2, cubes, metas, wide), f32),
            pltpu.VMEM(unit, bf),
            pltpu.VMEM((cubes, metas, wide), f32),
            pltpu.VMEM((owners, keys, width), f32),
            pltpu.VMEM((owners, keys, width), f32),
            pltpu.VMEM((line, slots, rows, width), bf),
            pltpu.VMEM((line, slots, rows, width), bf),
            pltpu.VMEM((line, slots, rows, width), bf),
            pltpu.VMEM((2 * slots + 2 * ends * CAP + 1, rows, width), bf),
            pltpu.VMEM((line, heads, piece, rows, width), bf),
            pltpu.VMEM((owners, *unit), bf),
            pltpu.VMEM((*pair, CAP, 2, rows, width), bf),
            pltpu.VMEM((*pair, 4, wide), f32),
            pltpu.VMEM((*pair, CAP, 2, rows, width), bf),
            pltpu.VMEM((*pair, 4, wide), f32),
            pltpu.VMEM((*pair, CAP, rows, width), bf),
            pltpu.VMEM((*pair, CAP, rows, width), bf),
            pltpu.VMEM((2, *unit), bf),
            dma((6,)),
            dma((heads, 2)), dma((heads, side_len, 2)), dma((line, heads, 2)), dma((line, heads, 2)),
            dma((line, heads, 2)), dma((line, heads, 2)),
            dma((side_len,)), dma((line,)), dma((line,)), dma((line,)), dma((line,)),
            dma((line,)), dma((line,)), dma((1,)), dma((1,)),
            dma((heads,)), dma((heads,)),
            dma((heads, 3)), dma((owners, heads)),
            dma((line,)), dma((line,)),
            dma((line, heads)), dma((side_len + 1, heads)), dma((owners, heads)), dma((heads,)),
            dma(pair), dma(pair), dma(pair), dma(pair), dma(pair), dma(pair),
            dma((2, heads)),
        ],
        compiler_params=pltpu.CompilerParams(
            collective_id=0, has_side_effects=True),
    )(
        chosen_cubes, chosen_owner.T, cubed(query_rows), cubed(key_rows), cubed(value_rows),
        cubed(output_grad), cubed(output_rows),
        row_logsumexp.reshape(1, tokens),
    )
    outs = pl.pallas_call(
        place,
        out_shape=[jax.ShapeDtypeStruct((piece, rows, full), bf)] * 3,
        in_specs=[vmem] * 2,
        out_specs=[vmem] * 3,
    )(*outs)
    return tuple(a.reshape(1, 1, piece_rows, full) for a in outs)


def solution(mesh):
    rows = P("seq", "head", None, None)
    return jax.shard_map(
        on_device,
        mesh=mesh,
        in_specs=(rows, rows, rows, rows, rows, P("seq", "head"), P("seq", None), P("seq", None, None)),
        out_specs=(rows, rows, rows),
        check_vma=False,
    )
```

```python
import functools
import math

import jax
import jax.numpy as jnp
from jax import lax
from jax.experimental import pallas as pl
from jax.experimental.pallas import tpu as pltpu
from jax.sharding import PartitionSpec as P

CAP = 2
PAIR = 2
SHARE = 2
LOG2E = math.log2(math.e)
NT = (((1,), (1,)), ((), ()))
NN = (((1,), (0,)), ((), ()))


def kernel(
    heads, seqs, sel,
    pick_ref, table_ref, q_ref, k_ref, v_ref, g_ref, o_ref, lse_ref,
    retq_ref, retkv_ref,
    qb, kv, kt, g_all, o_all, dsend, dlt, base, meta, tab, tab_s,
    slot, ret_ix, wq, wm, wy, wym, dk, dv, own_dq, give, got, wr, fin, skv,
    ys, ym, yr, yrm, yd, yq, part,
    loc_sem, qx_s, qn_s, qg_s, q_r, qc_s, qc_r, mn_s, mg_s, m_r, mc_s, mc_r,
    t_s, t_r, tc_s, tc_r, dl_s, dl_r, kv_s, kv_r, gv_s, gv_r, fq_s, fq_r, fk_s, fk_r,
    ys_s, ys_r, ym_s, ym_r, yd_s, yd_r, part_r,
):
    h = lax.axis_index("head")
    s = lax.axis_index("seq")
    group = PAIR * SHARE
    line = seqs // group
    z = s // group
    y = (s // PAIR) % SHARE
    c = s % PAIR
    side_len = line // 2
    ends = side_len - 1
    side = z // side_len
    first = side * side_len
    _, _, _, _, piece, rows, width = qb.shape
    cubes = heads * piece
    keys = cubes * rows
    wide = CAP * rows
    metas = meta.shape[3]
    scale = 1.0 / math.sqrt(width)
    gate_here = (1 - side) * (side_len - 1) + side * side_len
    gate_far = (1 - side) * side_len + side * (side_len - 1)
    is_gate = z == gate_here
    is_end = z != gate_here
    owners = 2 + ends
    finds = owners + 2 * ends
    own_slots = owners * CAP
    zero_slot = 2 * own_slots + 2 * ends * CAP

    def dev(hh, zz, yy, cc):
        return {"head": hh, "seq": zz * group + yy * PAIR + cc}

    def near(t):
        return first + (z - first + t) % side_len

    def source(t):
        is_far = t // side_len
        k = t - side_len
        far = (1 - side) * (side_len + k) + side * (side_len - 1 - k)
        return (1 - is_far) * near(t) + is_far * far

    def other(t):
        return (h + t) % heads

    barrier = pltpu.get_barrier_semaphore()
    for t in range(heads):
        pl.semaphore_signal(barrier, inc=1, device_id=dev(other(t), z, 1 - y, c))
        for m in range(line):
            if t or m:
                pl.semaphore_signal(barrier, inc=1, device_id=dev(other(t), (z + m) % line, y, c))
    pl.semaphore_signal(barrier, inc=1, device_id=dev(h, z, y, 1 - c))
    pl.semaphore_signal(barrier, inc=1, device_id=dev(h, z, 1 - y, 1 - c))
    partners = heads + heads * line + 1

    def cols(a):
        return pl.ds(pl.multiple_of(a * width, width), width)

    def rows_of(a):
        return pl.ds(a * piece, piece)

    loads = [pltpu.make_async_copy(g_ref, g_all, loc_sem.at[0]),
             pltpu.make_async_copy(o_ref, o_all, loc_sem.at[1])]
    stage = []
    for n, (a, b) in enumerate(((q_ref, k_ref), (g_ref, v_ref))):
        stage.append(pltpu.make_async_copy(a.at[:, :, cols(h)], qb.at[0, z, h, n], loc_sem.at[2 + n]))
        stage.append(pltpu.make_async_copy(b.at[:, :, cols(h)], kv.at[0, h, n], loc_sem.at[4 + n]))
    for d in loads + stage:
        d.start()

    pl.semaphore_wait(barrier, partners)

    def remote(src, dst, send, recv, to):
        return pltpu.make_async_remote_copy(
            src_ref=src, dst_ref=dst, send_sem=send, recv_sem=recv, device_id=to)

    def hop(m):
        return gate_far if m == 0 else near(m)

    def q_own(p, m, n):
        return remote(qb.at[0, z, p, n], qb.at[0, z, p, n], qn_s.at[p, m, n], q_r.at[z, p, n], dev(h, hop(m), y, c))

    def q_relay(zz, p, n):
        return remote(qb.at[0, zz, p, n], qb.at[0, zz, p, n], qg_s.at[zz, p, n], q_r.at[zz, p, n],
                      dev(h, gate_far, y, c))

    def q_cross(t, n):
        a = other(t)
        return remote(qb.at[0, z, a, n], qb.at[0, z, h, n], qx_s.at[t, n], q_r.at[z, h, n], dev(a, z, y, c))

    def q_core(zz, p, n):
        return remote(qb.at[0, zz, p, n], qb.at[1, zz, p, n], qc_s.at[zz, p, n], qc_r.at[zz, p, n],
                      dev(h, z, y, 1 - c))

    def m_own(m):
        return remote(meta.at[0, z], meta.at[0, z], mn_s.at[m], m_r.at[z], dev(h, hop(m), y, c))

    def m_relay(zz):
        return remote(meta.at[0, zz], meta.at[0, zz], mg_s.at[zz], m_r.at[zz], dev(h, gate_far, y, c))

    def m_core(zz):
        return remote(meta.at[0, zz], meta.at[1, zz], mc_s.at[zz], mc_r.at[zz], dev(h, z, y, 1 - c))

    def t_line(m):
        return remote(table_ref, tab.at[0, z], t_s.at[m], t_r.at[z], dev(h, (z + m) % line, y, c))

    def t_from(zz):
        return remote(table_ref, tab.at[0, zz], t_s.at[0], t_r.at[zz], dev(h, zz, y, c))

    t_core = remote(tab.at[0], tab.at[1], tc_s.at[0], tc_r.at[0], dev(h, z, y, 1 - c))

    def d_cross(t):
        a = other(t)
        return remote(dsend.at[a], dlt.at[rows_of(h)], dl_s.at[t], dl_r.at[h], dev(a, z, y, c))

    def d_from(a):
        return remote(dsend.at[a], dlt.at[rows_of(a)], dl_s.at[0], dl_r.at[a], dev(a, z, y, c))

    def kv_done(t, o):
        return remote(kv.at[0, h], kv.at[o, h], kv_s.at[t, o], kv_r.at[o, h], dev(other(t), z, 1 - y, c))

    def kv_from(a, o):
        return remote(kv.at[0, h], kv.at[o, a], kv_s.at[0, 0], kv_r.at[o, a], dev(h, z, 1 - y, c))

    def give_copy(zz, count):
        part = pl.ds(0, count)
        return remote(give.at[zz, part], got.at[zz, part], gv_s.at[zz], gv_r.at[zz], dev(h, z, y, 1 - c))

    def fq_copy(t, zz, at):
        a = other(t)
        return remote(fin.at[zz, a], retq_ref.at[at, h], fq_s.at[zz, t], fq_r.at[at, h], dev(a, zz, y, c))

    def fq_from(at, a):
        return remote(fin.at[z, a], retq_ref.at[at, a], fq_s.at[0, 0], fq_r.at[at, a], dev(a, gate_far, y, c))

    def fk_copy(t, o):
        a = other(t)
        to, kind = (dev(h, z, 1 - y, c), 0) if o == 1 else (dev(h, near(o - 1), y, c), 1)
        return remote(skv.at[o, a], part.at[kind, a], fk_s.at[o, t], part_r.at[kind, a], to)

    def fk_from(a, kind):
        return remote(skv.at[0, a], part.at[kind, a], fk_s.at[0, 0], part_r.at[kind, a], dev(h, z, 1 - y, c))

    def fk_cross(t):
        a = other(t)
        return remote(skv.at[0, a], retkv_ref.at[h], fk_s.at[0, t], fk_r.at[h], dev(a, z, y, c))

    def fk_done(a):
        return remote(skv.at[0, a], retkv_ref.at[a], fk_s.at[0, 0], fk_r.at[a], dev(a, z, y, c))

    def y_copy(k, m, cc):
        return (
            remote(ys.at[k, m, cc], yr.at[k, m, c], ys_s.at[k, m, cc], ys_r.at[k, m, c], dev(h, z, 1 - y, cc)),
            remote(ym.at[k, m, cc], yrm.at[k, m, c], ym_s.at[k, m, cc], ym_r.at[k, m, c], dev(h, z, 1 - y, cc)),
        )

    def y_from(k, m, cc):
        return (
            remote(ys.at[k, m, cc], yr.at[k, m, cc], ys_s.at[k, m, cc], ys_r.at[k, m, cc], dev(h, z, 1 - y, cc)),
            remote(ym.at[k, m, cc], yrm.at[k, m, cc], ym_s.at[k, m, cc], ym_r.at[k, m, cc], dev(h, z, 1 - y, cc)),
        )

    def y_back(k, m, cc):
        return remote(yd.at[k, m, cc], yq.at[k, m, c], yd_s.at[k, m, cc], yd_r.at[k, m, c], dev(h, z, 1 - y, cc))

    def y_done(k, m, cc):
        return remote(yd.at[k, m, cc], yq.at[k, m, cc], yd_s.at[k, m, cc], yd_r.at[k, m, cc], dev(h, z, 1 - y, cc))

    def send_parts(srcs, dst, send, recv, a, to):
        for n, src in enumerate(srcs):
            remote(src.at[:, :, cols(a)], dst.at[n], send, recv, to).start()

    def send_q(dst, send, recv, a, to):
        for n, src in enumerate((q_ref, g_ref)):
            remote(src.at[:, :, cols(a)], dst.at[n], send.at[n], recv.at[n], to).start()

    def first_part(m):
        send_q(qb.at[0, z, h], qn_s.at[h, m], q_r.at[z, h], h, dev(h, hop(m), y, c))

    for m in range(1, line):
        t_line(m).start()

    @pl.when(is_gate)
    def _():
        first_part(0)

    for m in range(1, side_len):
        first_part(m)
    for t in range(1, heads):
        send_q(qb.at[0, z, h], qx_s.at[t], q_r.at[z, h], other(t), dev(other(t), z, y, c))
    send_q(qb.at[1, z, h], qc_s.at[z, h], qc_r.at[z, h], h, dev(h, z, y, 1 - c))

    row = lax.broadcasted_iota(jnp.int32, (metas, wide), 0)
    lane = lax.broadcasted_iota(jnp.int32, (3, wide), 1)
    for d in loads:
        d.wait()
    for a in range(heads):
        for x in range(piece):
            prod = g_all[x, :, a * width:(a + 1) * width].astype(jnp.float32) * o_all[
                x, :, a * width:(a + 1) * width
            ].astype(jnp.float32)
            both = jnp.concatenate([prod] * CAP, axis=0)
            total = jnp.sum(both.T, axis=0, keepdims=True)
            dsend[a, x] = jnp.where(row == 1, jnp.broadcast_to(total, (metas, wide)), 0.0)
    for t in range(1, heads):
        d_cross(t).start()
    for t in range(heads):
        for o in (1, 0):
            if t or o:
                send_parts((k_ref, v_ref), kv.at[o, h], kv_s.at[t, o], kv_r.at[o, h], other(t),
                           dev(other(t), z, (y + o) % SHARE, c))

    for x in range(cubes):
        line_x = jnp.concatenate([lse_ref[:, x * rows:(x + 1) * rows] * LOG2E] * CAP, axis=1)
        both = jnp.where(row == 0, jnp.broadcast_to(line_x, (metas, wide)), 0.0)
        for j in range(sel):
            bits = jnp.int32(0)
            for k in range(cubes):
                bits = bits + jnp.where(pick_ref[x, j, k] != 0, 1 << k, 0)
            both = jnp.where(row == 2 + j, bits.astype(jnp.float32), both)
        base[x] = both
    tab[0, z] = table_ref[...]
    dlt[rows_of(h)] = dsend[h]
    for d in stage:
        d.wait()

    def recv_part(t, i, relays):
        zz = source(t)
        p = other(i)
        for n in range(2):
            q_relay(zz, p, n).wait_recv()
            if relays:
                q_relay(zz, p, n).start()
            q_core(zz, p, n).start()

    def recv_meta(t, relays):
        zz = source(t)
        m_relay(zz).wait_recv()
        if relays:
            m_relay(zz).start()
        m_core(zz).start()

    for t in range(1, heads):
        for n in range(2):
            q_relay(z, other(t), n).wait_recv()

            @pl.when(is_gate)
            def _():
                q_own(other(t), 0, n).start()

            for m in range(1, side_len):
                q_own(other(t), m, n).start()
            q_core(z, other(t), n).start()

    @pl.when(is_gate)
    def _():
        for t in range(1, side_len):
            recv_part(t, 0, True)

    for t in range(1, heads):
        d_from(other(t)).wait_recv()
    for x in range(cubes):
        meta[0, z, x] = base[x] + dlt[x]

    @pl.when(is_gate)
    def _():
        m_own(0).start()

    for m in range(1, side_len):
        m_own(m).start()
    m_core(z).start()

    @pl.when(is_end)
    def _():
        at = 1 + (z - gate_here + side_len) % side_len
        for t in range(heads):
            send_parts((k_ref, v_ref), kv.at[at, h], kv_s.at[t, 2], kv_r.at[at, h], other(t),
                       dev(other(t), gate_here, y, c))

    dk[...] = jnp.zeros_like(dk)
    dv[...] = jnp.zeros_like(dv)
    wr[zero_slot] = jnp.zeros_like(wr[zero_slot])

    for m in range(1, line):
        t_from((z + m) % line).wait_recv()
    t_core.start()

    t_core.wait_recv()
    to_smem = pltpu.make_async_copy(tab, tab_s, loc_sem.at[0])
    to_smem.start()
    to_smem.wait()

    def number(zz, yy, cc):
        return zz * group + yy * PAIR + cc

    mine = [number(z, y, c), number(z, 1 - y, c)]
    mine = mine + [number(near(m), y, c) for m in range(1, side_len)]
    across = [number(near(m), 1 - y, cc) for m in range(1, side_len) for cc in range(PAIR)]
    theirs = [number(z, y, 1 - c), number(z, 1 - y, 1 - c)]
    theirs = theirs + [number(near(m), y, 1 - c) for m in range(1, side_len)]

    def find(zz, l, who):
        for o, d in who:
            found = [jnp.int32(-1)] * CAP
            for e in range(cubes * sel - 1, -1, -1):
                hit = tab_s[l, zz, e % sel, e // sel] == d
                for k in range(CAP - 1, 0, -1):
                    found[k] = jnp.where(hit, found[k - 1], found[k])
                found[0] = jnp.where(hit, e, found[0])
            for k in range(CAP):
                slot[((zz * 2 + l) * finds + o) * CAP + k] = found[k]

    def rank(zz, who):
        count = [jnp.int32(0)] * len(who)
        for e in range(cubes * sel):
            d = tab_s[0, zz, e % sel, e // sel]
            ix = jnp.int32(zero_slot)
            for n, (at, d_n) in enumerate(who):
                hit = d == d_n
                ix = jnp.where(hit, at + jnp.minimum(count[n], CAP - 1), ix)
                count[n] = count[n] + hit.astype(jnp.int32)
            ret_ix[zz * cubes * sel + e] = ix

    @pl.loop(0, side_len)
    def _(t):
        zz = source(t)
        for l in range(2):
            find(zz, l, list(enumerate(mine[:2])))
        rank(zz, [(o * CAP, d) for o, d in enumerate(mine[:2])]
             + [(own_slots + o * CAP, d) for o, d in enumerate(theirs[:2])])

    @pl.when(is_gate)
    def _():
        @pl.loop(side_len, line)
        def _(t):
            zz = source(t)
            find(zz, 0, list(enumerate(mine + across)))
            find(zz, 1, list(enumerate(mine)))
            rank(zz, [(o * CAP, d) for o, d in enumerate(mine)]
                 + [(own_slots + o * CAP, d) for o, d in enumerate(theirs)]
                 + [(2 * own_slots + o * CAP, d) for o, d in enumerate(across)])

    @pl.when(is_gate)
    def _():
        for t in range(1, side_len):
            for i in range(1, heads):
                recv_part(t, i, True)
            recv_meta(t, True)

    @pl.when(is_end)
    def _():
        for t in range(1, side_len):
            for i in range(heads):
                recv_part(t, i, False)
            recv_meta(t, False)

    def stage_far(k):
        zz = source(side_len + k)
        for i in range(heads):
            recv_part(side_len + k, i, False)
        recv_meta(side_len + k, False)
        wy[...] = qb[0, zz]
        wym[...] = meta[0, zz]
        for m in range(ends):
            for cc in range(PAIR):
                es = [slot[(zz * 2 * finds + owners + m * PAIR + cc) * CAP + n] for n in range(CAP)]
                ym[k, m, cc] = jnp.concatenate([info(wym, es), jnp.zeros((1, wide), jnp.float32)], axis=0)
                for n in range(CAP):
                    x = lax.div(jnp.maximum(es[n], 0), sel)
                    ys[k, m, cc, n] = wy[lax.div(x, piece), :, lax.rem(x, piece)]
                for d in y_copy(k, m, cc):
                    d.start()

    def info(table, es):
        out = None
        for n in range(CAP):
            e = jnp.maximum(es[n], 0)
            m = table[lax.div(e, sel)]
            bits = jnp.zeros_like(m[0:1])
            for j in range(sel):
                bits = jnp.where((es[n] >= 0) & (lax.rem(e, sel) == j), m[2 + j:3 + j], bits)
            one = jnp.concatenate([m[0:2], bits], axis=0)
            out = one if n == 0 else jnp.where(lane < n * rows, out, one)
        return out

    @pl.when(is_gate)
    def _():
        stage_far(0)

    for a in range(heads):
        for o in range(2):
            if a or o:
                kv_from(other(a), o).wait_recv()
    for o in range(2):
        kt[o] = kv[o, :, 0].reshape(keys, width).astype(jnp.float32).T.astype(jnp.bfloat16)
    bit = lax.broadcasted_iota(jnp.int32, (cubes, 2 * wide), 0)

    def compute(o, qs, gs, both):
        kept = (both[2:3].astype(jnp.int32) >> bit) & 1
        lines = jnp.where(kept == 1, both[0:1], jnp.inf)
        kk = kv[o, :, 0].reshape(keys, width)
        vv = kv[o, :, 1].reshape(keys, width)
        st = lax.dot_general(kk, qs, NT, preferred_element_type=jnp.float32)
        dpt = lax.dot_general(vv, gs, NT, preferred_element_type=jnp.float32)
        st = st.reshape(cubes, rows, 2 * wide)
        p = jnp.exp2(st * (scale * LOG2E) - lines[:, None, :])
        ds = p * (dpt.reshape(cubes, rows, 2 * wide) - both[1:2][:, None, :])
        pb = p.astype(jnp.bfloat16).reshape(keys, 2 * wide)
        dsb = ds.astype(jnp.bfloat16).reshape(keys, 2 * wide)
        dv[o] += lax.dot_general(pb, gs, NN, preferred_element_type=jnp.float32)
        dk[o] += lax.dot_general(dsb, qs, NN, preferred_element_type=jnp.float32)
        dqt = lax.dot_general(kt[o], dsb, NN, preferred_element_type=jnp.float32)
        return (dqt.T * scale).astype(jnp.bfloat16).reshape(2, CAP, rows, width)

    def work(zz, o):
        es = [[slot[((zz * 2 + l) * finds + o) * CAP + k] for k in range(CAP)] for l in range(2)]
        xs = [(l, lax.div(jnp.maximum(e, 0), sel)) for l in range(2) for e in es[l]]
        qs = jnp.concatenate([wq[l, lax.div(x, piece), 0, lax.rem(x, piece)] for l, x in xs], axis=0)
        gs = jnp.concatenate([wq[l, lax.div(x, piece), 1, lax.rem(x, piece)] for l, x in xs], axis=0)
        both = jnp.concatenate([info(wm.at[0], es[0]), info(wm.at[1], es[1])], axis=1)
        dq = compute(o, qs, gs, both)
        own_dq[zz, o * CAP:(o + 1) * CAP] = dq[0]
        give[zz, o * CAP:(o + 1) * CAP] = dq[1]

    def works(t, many):
        zz = source(t)
        for p in range(heads):
            for n in range(2):
                q_core(zz, p, n).wait_recv()
        m_core(zz).wait_recv()
        for l in range(2):
            wq[l] = qb[l, zz]
            wm[l] = meta[l, zz]
        for o in range(many):
            work(zz, o)
        give_copy(zz, many * CAP).start()

    def finish(t, many):
        zz = source(t)
        give_copy(zz, many * CAP).wait_recv()
        wr[0:many * CAP] = own_dq[zz, 0:many * CAP]
        wr[own_slots:own_slots + many * CAP] = got[zz, 0:many * CAP]
        if many > 2:
            k = t - side_len
            for m in range(ends):
                for cc in range(PAIR):
                    y_done(k, m, cc).wait_recv()
                    at = 2 * own_slots + (m * PAIR + cc) * CAP
                    wr[at:at + CAP] = yq[k, m, cc]
        at = side_len if many > 2 else z - first
        for i in later + [0]:
            a = other(i)
            for x in range(piece):
                e = (zz * cubes + a * piece + x) * sel
                total = wr[ret_ix[e]].astype(jnp.float32)
                for j in range(1, sel):
                    total = total + wr[ret_ix[e + j]].astype(jnp.float32)
                fin[zz, a, x] = total.astype(jnp.bfloat16)
            if i or many > 2:
                fq_copy(i, zz, at).start()
            else:
                @pl.when(zz != z)
                def _():
                    fq_copy(0, zz, at).start()

    def span(a):
        return pl.ds(pl.multiple_of(a * piece * rows, piece * rows), piece * rows)

    def give_part(t, o):
        a = other(t)
        for n, total in enumerate((dk[o, span(a)] * scale, dv[o, span(a)])):
            skv[o, a, n] = total.astype(jnp.bfloat16).reshape(piece, rows, width)
        fk_copy(t, o).start()

    def total_part(t, kinds):
        a = other(t)
        for kind in range(kinds):
            fk_from(a, kind).wait_recv()
        for n, total in enumerate((dk[0, span(a)] * scale, dv[0, span(a)])):
            total = total.reshape(piece, rows, width)
            for kind in range(kinds):
                total = total + part[kind, a, n].astype(jnp.float32)
            skv[0, a, n] = total.astype(jnp.bfloat16)
        if t:
            fk_cross(t).start()
        else:
            keep_k.start()

    later = list(range(1, heads))
    keep_q = pltpu.make_async_copy(fin.at[z, h], retq_ref.at[z - first, h], loc_sem.at[1])
    keep_k = pltpu.make_async_copy(skv.at[0, h], retkv_ref.at[h], loc_sem.at[2])

    @pl.loop(0, side_len)
    def _(t):
        works(t, 2)

    @pl.when(is_gate)
    def _():
        for k in range(1, min(2, side_len)):
            stage_far(k)
        for m in range(ends):
            for a in range(heads):
                kv_from(a, 2 + m).wait_recv()
            kt[2 + m] = kv[2 + m, :, 0].reshape(keys, width).astype(jnp.float32).T.astype(jnp.bfloat16)

    @pl.loop(0, side_len)
    def _(t):
        finish(t, 2)

    keep_q.start()

    @pl.when(is_end)
    def _():
        for t in later + [0]:
            give_part(t, 1)
        for t in later + [0]:
            total_part(t, 2)

    @pl.when(is_gate)
    def _():
        def across_work(t):
            k = t - side_len
            for m in range(ends):
                for cc in range(PAIR):
                    for d in y_from(k, m, cc):
                        d.wait_recv()
                at = [(cc, n) for cc in range(PAIR) for n in range(CAP)]
                qs = jnp.concatenate([yr[k, m, cc, n, 0] for cc, n in at], axis=0)
                gs = jnp.concatenate([yr[k, m, cc, n, 1] for cc, n in at], axis=0)
                both = jnp.concatenate([yrm[k, m, cc] for cc in range(PAIR)], axis=1)
                dq = compute(2 + m, qs, gs, both)
                for cc in range(PAIR):
                    yd[k, m, cc] = dq[cc]
                    y_back(k, m, cc).start()

        @pl.loop(side_len, line)
        def _(t):
            works(t, owners)

            @pl.when(t + 2 < line)
            def _():
                stage_far(t + 2 - side_len)

            across_work(t)

            @pl.when((t > side_len) & (t + 1 < line))
            def _():
                finish(t - 1, owners)

        for m in range(ends):
            for t in later + [0]:
                give_part(t, 2 + m)
        for t in later + [0]:
            give_part(t, 1)
        finish(line - 2, owners)
        finish(line - 1, owners)
        for t in later + [0]:
            total_part(t, 1)

    for m in range(1, side_len):
        for p in range(heads):
            for n in range(2):
                q_own(p, m, n).wait_send()
        m_own(m).wait_send()
    for t in range(1, heads):
        for n in range(2):
            q_cross(t, n).wait_send()
        d_cross(t).wait_send()
        kv_done(t, 0).wait_send()
    for t in range(heads):
        kv_done(t, 1).wait_send()
    for m in range(1, line):
        t_line(m).wait_send()
    t_core.wait_send()

    @pl.loop(0, side_len)
    def _(t):
        zz = source(t)
        for p in range(heads):
            for n in range(2):
                q_core(zz, p, n).wait_send()
        m_core(zz).wait_send()
        give_copy(zz, 2 * CAP).wait_send()

    @pl.when(is_end)
    def _():
        for t in range(heads):
            kv_done(t, 2).wait_send()

    @pl.when(is_gate)
    def _():
        for p in range(heads):
            for n in range(2):
                q_own(p, 0, n).wait_send()
        m_own(0).wait_send()
        for t in range(1, side_len):
            for p in range(heads):
                for n in range(2):
                    q_relay(near(t), p, n).wait_send()
            m_relay(near(t)).wait_send()
        for t in range(side_len, line):
            k = t - side_len
            zz = source(t)
            for p in range(heads):
                for n in range(2):
                    q_core(zz, p, n).wait_send()
            m_core(zz).wait_send()
            give_copy(zz, owners * CAP).wait_send()
            for m in range(ends):
                for cc in range(PAIR):
                    for d in y_copy(k, m, cc):
                        d.wait_send()
                    y_back(k, m, cc).wait_send()
            for i in range(heads):
                fq_copy(i, zz, side_len).wait_send()
        for m in range(ends):
            for t in range(heads):
                fk_copy(t, 2 + m).wait_send()

    for t in range(heads):
        fk_copy(t, 1).wait_send()
        if t:
            fk_cross(t).wait_send()
            fk_done(other(t)).wait_recv()
        for m in range(side_len):
            if t or m:
                zz = near(m)
                fq_copy(t, zz, z - first).wait_send()
                fq_from(zz - first, other(t)).wait_recv()
        fq_from(side_len, other(t)).wait_recv()
    keep_q.wait()
    keep_k.wait()


def place(q_ref, kv_ref, oq_ref, ok_ref, ov_ref):
    line, heads, piece, rows, width = q_ref.shape
    for a in range(heads):
        at = slice(a * width, (a + 1) * width)
        total = q_ref[0, a].astype(jnp.float32)
        for m in range(1, line):
            total = total + q_ref[m, a].astype(jnp.float32)
        oq_ref[:, :, at] = total.astype(jnp.bfloat16)
        for n, out in enumerate((ok_ref, ov_ref)):
            out[:, :, at] = kv_ref[a, n]


def on_device(
    query_rows, key_rows, value_rows, output_grad, output_rows, row_logsumexp,
    chosen_owner, chosen_cubes,
):
    heads = lax.axis_size("head")
    seqs = lax.axis_size("seq")
    piece_rows, full = query_rows.shape[2:]
    width = full // heads
    cubes, sel = chosen_owner.shape
    tokens = row_logsumexp.shape[0]
    rows = tokens // cubes
    piece = piece_rows // rows
    wide = CAP * rows
    line = seqs // (PAIR * SHARE)
    side_len = line // 2
    keys = cubes * rows
    metas = 2 + sel

    def cubed(a):
        return a.reshape(piece, rows, full)

    bf, f32, i32 = jnp.bfloat16, jnp.float32, jnp.int32
    vmem = pl.BlockSpec(memory_space=pltpu.VMEM)
    anywhere = pl.BlockSpec(memory_space=pl.ANY)
    smem = pl.BlockSpec(memory_space=pltpu.SMEM)
    dma = pltpu.SemaphoreType.DMA
    ends = side_len - 1
    owners = 2 + ends
    slots = owners * CAP
    finds = owners + PAIR * ends
    unit = (heads, 2, piece, rows, width)
    pair = (side_len, ends, PAIR)
    outs = pl.pallas_call(
        functools.partial(kernel, heads, seqs, sel),
        out_shape=[
            pltpu.VMEM((side_len + 1, heads, piece, rows, width), bf),
            pltpu.VMEM(unit, bf),
        ],
        in_specs=[smem, vmem] + [anywhere] * 5 + [vmem],
        out_specs=[vmem] * 2,
        scratch_shapes=[
            pltpu.VMEM((2, line, *unit), bf),
            pltpu.VMEM((owners, *unit), bf),
            pltpu.VMEM((owners, width, keys), bf),
            pltpu.VMEM((piece, rows, full), bf),
            pltpu.VMEM((piece, rows, full), bf),
            pltpu.VMEM((heads, piece, metas, wide), f32),
            pltpu.VMEM((cubes, metas, wide), f32),
            pltpu.VMEM((cubes, metas, wide), f32),
            pltpu.VMEM((2, line, cubes, metas, wide), f32),
            pltpu.VMEM((2, line, sel, cubes), i32),
            pltpu.SMEM((2, line, sel, cubes), i32),
            pltpu.SMEM((line * 2 * finds * CAP,), i32),
            pltpu.SMEM((line * cubes * sel,), i32),
            pltpu.VMEM((2, *unit), bf),
            pltpu.VMEM((2, cubes, metas, wide), f32),
            pltpu.VMEM(unit, bf),
            pltpu.VMEM((cubes, metas, wide), f32),
            pltpu.VMEM((owners, keys, width), f32),
            pltpu.VMEM((owners, keys, width), f32),
            pltpu.VMEM((line, slots, rows, width), bf),
            pltpu.VMEM((line, slots, rows, width), bf),
            pltpu.VMEM((line, slots, rows, width), bf),
            pltpu.VMEM((2 * slots + 2 * ends * CAP + 1, rows, width), bf),
            pltpu.VMEM((line, heads, piece, rows, width), bf),
            pltpu.VMEM((owners, *unit), bf),
            pltpu.VMEM((*pair, CAP, 2, rows, width), bf),
            pltpu.VMEM((*pair, 4, wide), f32),
            pltpu.VMEM((*pair, CAP, 2, rows, width), bf),
            pltpu.VMEM((*pair, 4, wide), f32),
            pltpu.VMEM((*pair, CAP, rows, width), bf),
            pltpu.VMEM((*pair, CAP, rows, width), bf),
            pltpu.VMEM((2, *unit), bf),
            dma((6,)),
            dma((heads, 2)), dma((heads, side_len, 2)), dma((line, heads, 2)), dma((line, heads, 2)),
            dma((line, heads, 2)), dma((line, heads, 2)),
            dma((side_len,)), dma((line,)), dma((line,)), dma((line,)), dma((line,)),
            dma((line,)), dma((line,)), dma((1,)), dma((1,)),
            dma((heads,)), dma((heads,)),
            dma((heads, 3)), dma((owners, heads)),
            dma((line,)), dma((line,)),
            dma((line, heads)), dma((side_len + 1, heads)), dma((owners, heads)), dma((heads,)),
            dma(pair), dma(pair), dma(pair), dma(pair), dma(pair), dma(pair),
            dma((2, heads)),
        ],
        compiler_params=pltpu.CompilerParams(
            collective_id=0, has_side_effects=True),
    )(
        chosen_cubes, chosen_owner.T, cubed(query_rows), cubed(key_rows), cubed(value_rows),
        cubed(output_grad), cubed(output_rows),
        row_logsumexp.reshape(1, tokens),
    )
    outs = pl.pallas_call(
        place,
        out_shape=[jax.ShapeDtypeStruct((piece, rows, full), bf)] * 3,
        in_specs=[vmem] * 2,
        out_specs=[vmem] * 3,
    )(*[pltpu.with_memory_space_constraint(a, pltpu.VMEM) for a in outs])
    return tuple(a.reshape(1, 1, piece_rows, full) for a in outs)


def solution(mesh):
    rows = P("seq", "head", None, None)
    return jax.shard_map(
        on_device,
        mesh=mesh,
        in_specs=(rows, rows, rows, rows, rows, P("seq", "head"), P("seq", None), P("seq", None, None)),
        out_specs=(rows, rows, rows),
        check_vma=False,
    )
```
